512 devices in a mesh: seq: 64 (over z, x), tp: 8 (over y, core).
Axes of the slice: x: 4, y: 4, z: 16, core: 2. Of those that a mesh axis runs over, the one named last changes fastest.
Arguments:
- latent: bfloat16 [16384, 5120], P('seq', 'tp'), may hold values from -12 to 12
- pose_rows: bfloat16 [16384, 256], P('seq'), may hold values from -6 to 6
- dest_device: int32 [16384, 1], P('seq'), may hold values from 0 to 63; in each aligned block of 256 rows (0 to 255, 256 to 511, ...) at most 8 rows name the same one
- dest_slot: int32 [16384], P('seq'), may hold values from 0 to 255
- w_section1: bfloat16 [16, 32], replicated, may hold values from -1.5 to 1.5
- w_section2: bfloat16 [128, 128], replicated, may hold values from -0.5 to 0.5
- w_section3: bfloat16 [512, 5120], P(None, 'tp'), may hold values from -0.25 to 0.25
- shift_mod: float32 [5120], P('tp'), may hold values from -3 to 3
- scale_mod: float32 [5120], P('tp'), may hold values from -0.5 to 0.5
- w_query: bfloat16 [5120, 5120], P('seq', 'tp'), may hold values from -0.078125 to 0.078125
- bias_query: float32 [5120], P('tp'), may hold values from -3 to 3
- gain_query: float32 [5120], P('tp'), may hold values from 0.25 to 1.75
- cotangent: bfloat16 [16384, 5120], P('seq', 'tp'), may hold values from -16 to 16
Outputs:
- normed_query: bfloat16 [16384, 5120], P('seq', 'tp')
- section_three_grad: float32 [512, 5120], P('seq', 'tp')
- section_two_grad: float32 [128, 128], replicated
- section_one_grad: float32 [16, 32], replicated
The draws below stay inside these ranges and needn't reach their ends.
Inputs may be any that keep to these rules, and one draw needn't show every extreme that they name: `dest_device`: among the rows of one device no index of seq appears more than 8 times, and some index appears exactly 8 times among some device's rows.
All inputs are finite; a program needn't handle non-finite values.
Results may differ from the reference program's by a relative error of at most 0.02.
Values may be sent and summed in bfloat16 or wider, within the bound.
No kernel may reach another device: no remote copies, remote signals or barrier semaphores. Data moves between devices by JAX's collectives and lax.ppermute only.
A program may use at most 64 MiB of HBM per device.

```python
import math
import jax
import jax.numpy as jnp
import numpy as np
from jax import lax

D = 5120
C1 = 32
C2 = 128
TOK_DEV = 256
TOKENS = 16384
ROWS = 16384
QW = 5120
CAP = 8
N_SEQ = 64
N_TP = 8


def draw_latent(key, part):
    key_base, key_col = jax.random.split(jax.random.fold_in(key, 11), 2)
    column = jnp.exp(math.log(0.3) + jax.random.uniform(key_col, (1, D), jnp.float32) * math.log(10.0))
    base = jax.random.normal(key_base, (TOKENS, D), jnp.float32)
    base = jnp.clip(base, -4.0, 4.0)
    return (base * column).astype(jnp.bfloat16)


def draw_cotangent(key, part):
    key_base = jax.random.fold_in(key, 23)
    place = jnp.arange(TOKENS, dtype=jnp.float32)[:, None] / max(TOKENS - 1, 1)
    base = jnp.clip(jax.random.normal(key_base, (TOKENS, QW), jnp.float32), -4.0, 4.0)
    rising = 1.0 + 2.0 * place
    return (base * rising * (1.0 / math.sqrt(TOKENS))).astype(jnp.bfloat16)


def with_ends(values, rng, least, top_value):
    spot = [jax.random.randint(jax.random.fold_in(rng, axis), (), 0, length) for axis, length in enumerate(values.shape)]
    widest = values.shape.index(max(values.shape))
    beside = spot[:widest] + [(spot[widest] + 1) % values.shape[widest]] + spot[widest + 1:]
    return values.at[tuple(spot)].set(least).at[tuple(beside)].set(top_value)


def levels(stream_key, extent, shards, least, largest):
    factor_of, own = 1.0, jax.random.fold_in(stream_key, 6)
    for dim, parts in shards:
        heights = jnp.exp(jax.random.uniform(jax.random.fold_in(own, dim), (parts,), jnp.float32, least / len(shards), largest / len(shards)))
        factor_of = factor_of * jnp.repeat(heights, extent[dim] // parts).reshape([-1 if axis == dim else 1 for axis in range(len(extent))])
    return factor_of


def deal_out(stream_key, own, number, rows, number_of, top, bound, lean):
    order = jax.random.permutation(stream_key, number_of)
    crowded, ordinary = load_shares(number_of, rows * top, bound, lean, True), load_shares(number_of, rows * top, bound, lean, False)
    places = jnp.arange(number_of)

    def named(lengths, rotation):
        used = int((lengths > 0).sum())
        fixed = max(1, used // 4)
        moved = fixed + (places - fixed + rotation * (used - fixed)) % max(1, number_of - fixed)
        return jnp.zeros((number_of,), jnp.int32).at[order[jnp.where(places < fixed, places, moved)]].set(jnp.asarray(lengths, jnp.int32))

    lengths = jnp.where(number % 4 == 0, named(crowded, number // 4), named(ordinary, number - number // 4 - 1))
    mixed = jax.random.permutation(jax.random.fold_in(own, 3), number_of)
    giver, taker = mixed[0:number_of // 2 * 2:2], mixed[1:number_of // 2 * 2:2]
    slack = jnp.minimum(lengths[giver] - 1, bound - lengths[taker]) // 2
    slack = jnp.where((giver == order[0]) | (taker == order[0]) | (lengths[taker] == 0), 0, jnp.maximum(slack, 0))
    moved = jax.random.randint(jax.random.fold_in(own, 4), (number_of // 2,), 0, 1 << 20) % (slack + 1)
    lengths = lengths.at[giver].add(-moved).at[taker].add(moved)
    labels = jnp.searchsorted(jnp.cumsum(lengths), jnp.arange(rows * top), side="right").astype(jnp.int32)
    listing = labels.reshape(top, rows).T
    listing = listing[jax.random.permutation(jax.random.fold_in(own, 1), rows)]
    rotation = jax.random.randint(jax.random.fold_in(own, 2), (rows, 1), 0, top)
    return jnp.take_along_axis(listing, (jnp.arange(top)[None, :] + rotation) % top, axis=1)


def load_shares(amount, total, reach, skew, full):
    weights = [(1 << 20) // math.isqrt(standing ** skew) + 1 for standing in range(1, amount + 1)]
    largest = reach if full else min(reach, max(-(-total // amount), total * weights[0] // sum(weights)))
    least = 1 if total - largest >= amount - 1 else 0
    counts, spare = [largest] + [least] * (amount - 1), total - largest - least * (amount - 1)
    while spare > 0:
        free = [i for i in range(1, amount) if counts[i] < largest] or [i for i in range(1, amount) if counts[i] < reach]
        whole, budget = sum([weights[i] for i in free]), spare
        for i in free:
            more = min(reach - counts[i], max(1, budget * weights[i] // whole), spare)
            counts[i] = counts[i] + more
            spare = spare - more
    return np.array(counts)


def scatter_about(stream_key, dims, scale, bound, cuts=(), kind=jnp.bfloat16):
    array = jax.random.normal(stream_key, dims, jnp.float32) * scale
    if len(cuts) > 0:
        array = levels(stream_key, dims, cuts, -0.22, 0.18) * array
    return jnp.clip(array, min=-bound, max=bound).astype(kind)


def setup_inputs(seed: int = 0) -> dict:
    key_list = jax.random.split(jax.random.key(seed), 14)
    latent = draw_latent(jax.random.fold_in(key_list[13], 71), 0)
    pose_rows = scatter_about(key_list[1], (ROWS, 256), 1.5, 6.0, ((0, 64),))
    dest_device_keys = jax.random.split(jax.random.fold_in(key_list[2], 1), ROWS // TOK_DEV)
    dest_device_turns = jax.random.permutation(jax.random.fold_in(key_list[2], 3), ROWS // TOK_DEV)
    dest_device = jax.vmap(lambda own, number: deal_out(jax.random.fold_in(key_list[2], 2), own, number, TOK_DEV, N_SEQ, 1, CAP, 2))(dest_device_keys, dest_device_turns).reshape((ROWS, 1))
    dest_slot = with_ends(jax.random.randint(key_list[3], (ROWS,), 0, TOK_DEV), jax.random.fold_in(key_list[3], 1), 0, TOK_DEV - 1).astype(jnp.int32)
    w_section1 = scatter_about(key_list[4], (16, C1), 16 ** -0.5, 1.5)
    w_section2 = scatter_about(key_list[5], (4 * C1, C2), (4 * C1) ** -0.5, 0.5)
    w_section3 = scatter_about(key_list[6], (4 * C2, D), (4 * C2) ** -0.5, 0.25, ((1, 8),))
    shift_mod = scatter_about(key_list[7], (D,), 0.5, 3.0, ((0, 8),), jnp.float32)
    scale_mod = jnp.clip(jax.random.uniform(key_list[8], (D,), jnp.float32, -0.5, 0.5) * levels(key_list[8], (D,), ((0, 8),), -0.4, 0.0), -0.5, 0.5)
    w_query = scatter_about(key_list[9], (D, QW), D ** -0.5, 0.078125, ((0, 64), (1, 8)))
    bias_query = scatter_about(key_list[10], (QW,), 0.5, 3.0, ((0, 8),), jnp.float32)
    gain_query = jnp.clip(1.0 + 0.15 * jax.random.normal(key_list[11], (QW,), jnp.float32), 0.25, 1.75)
    cotangent = draw_cotangent(jax.random.fold_in(key_list[13], 71), 0)
    return {"latent": latent, "pose_rows": pose_rows, "dest_device": dest_device, "dest_slot": dest_slot, "w_section1": w_section1, "w_section2": w_section2, "w_section3": w_section3, "shift_mod": shift_mod, "scale_mod": scale_mod, "w_query": w_query, "bias_query": bias_query, "gain_query": gain_query, "cotangent": cotangent}


epsilon = 1e-06

def silu_slope(z):
    s = jax.nn.sigmoid(z)
    return s * (1.0 + z * (1.0 - s))

def run_sections(pose, w_one, w_two):
    count = pose.shape[0]
    c_one = w_one.shape[1]
    cells = pose.reshape(count * 16, 16)
    z_one = jnp.dot(cells, w_one, preferred_element_type=jnp.float32)
    feature_one = jax.nn.silu(z_one).astype(jnp.bfloat16)
    stacked_one = feature_one.reshape(count, 2, 2, 2, 2, c_one).transpose(0, 1, 3, 2, 4, 5).reshape(count * 4, 4 * c_one)
    z_two = jnp.dot(stacked_one, w_two, preferred_element_type=jnp.float32)
    stacked_two = jax.nn.silu(z_two).astype(jnp.bfloat16).reshape(count, 4 * w_two.shape[1])
    return (cells, z_one, stacked_one, z_two, stacked_two)

def section_back(cells, z_one, stacked_one, z_two, stacked_grad, w_two):
    quads = z_two.shape[0]
    count = quads // 4
    c_one = z_one.shape[1]
    two_grad = stacked_grad.reshape(quads, -1) * silu_slope(z_two)
    grad_two = lax.dot_general(stacked_one.astype(jnp.float32), two_grad, (((0,), (0,)), ((), ())), precision=lax.Precision.HIGHEST)
    back_one = jnp.dot(two_grad, w_two.astype(jnp.float32).T, precision=lax.Precision.HIGHEST)
    back_one = back_one.reshape(count, 2, 2, 2, 2, c_one).transpose(0, 1, 3, 2, 4, 5).reshape(count * 16, c_one)
    one_grad = back_one * silu_slope(z_one)
    grad_one = lax.dot_general(cells.astype(jnp.float32), one_grad, (((0,), (0,)), ((), ())), precision=lax.Precision.HIGHEST)
    return (grad_two, grad_one)

def reference(latent, pose_rows, dest_device, dest_slot, w_section1, w_section2, w_section3, shift_mod, scale_mod, w_query, bias_query, gain_query, cotangent):
    cells, z_one, stacked_one, z_two, stacked_two = run_sections(pose_rows, w_section1, w_section2)
    pose_tokens = jnp.dot(stacked_two, w_section3, preferred_element_type=jnp.float32).astype(jnp.bfloat16)
    target = (dest_device[:, 0] * TOK_DEV + dest_slot).astype(jnp.int32)
    guidance = jnp.zeros((TOKENS, D), jnp.float32).at[target].add(pose_tokens.astype(jnp.float32))
    summed = latent.astype(jnp.float32) + guidance
    center = lax.optimization_barrier(jnp.mean(summed, axis=1, keepdims=True))
    shifted = summed - center
    spread = lax.optimization_barrier(jnp.mean(shifted * shifted, axis=1, keepdims=True))
    inverse = lax.rsqrt(spread + epsilon)
    normed = shifted * inverse
    modulated = (normed * (1.0 + scale_mod) + shift_mod).astype(jnp.bfloat16)
    query = jnp.dot(modulated, w_query, preferred_element_type=jnp.float32) + bias_query
    rinv = lax.rsqrt(lax.optimization_barrier(jnp.mean(query * query, axis=1, keepdims=True)) + epsilon)
    normed_query = (query * rinv * gain_query).astype(jnp.bfloat16)
    upstream = cotangent.astype(jnp.float32) * gain_query
    along = lax.optimization_barrier(jnp.mean(upstream * query, axis=1, keepdims=True))
    query_grad = (upstream * rinv - query * along * rinv ** 3).astype(jnp.bfloat16)
    block_width = QW // N_TP
    modulated_grad = jnp.zeros((TOKENS, D), jnp.float32)
    for group in range(N_TP):
        lo_col = group * block_width
        term = jnp.dot(query_grad[:, lo_col:lo_col + block_width], w_query[:, lo_col:lo_col + block_width].T, preferred_element_type=jnp.float32)
        modulated_grad = modulated_grad + lax.optimization_barrier(term.astype(jnp.bfloat16)).astype(jnp.float32)
    normed_grad = modulated_grad * (1.0 + scale_mod)
    latent_grad = inverse * (normed_grad - lax.optimization_barrier(jnp.mean(normed_grad, axis=1, keepdims=True)) - normed * lax.optimization_barrier(jnp.mean(normed_grad * normed, axis=1, keepdims=True)))
    latent_grad = latent_grad.astype(jnp.bfloat16)
    row_grad = latent_grad[target]
    section_three_grad = lax.dot_general(stacked_two, row_grad, (((0,), (0,)), ((), ())), preferred_element_type=jnp.float32)
    stacked_grad = jnp.dot(row_grad, w_section3.T, preferred_element_type=jnp.float32)
    section_two_grad, section_one_grad = section_back(cells, z_one, stacked_one, z_two, stacked_grad, w_section2)
    return (normed_query, section_three_grad, section_two_grad, section_one_grad)
```

```python
import jax
import jax.numpy as jnp
from jax import lax
from jax.experimental import pallas as pl
from jax.experimental.pallas import tpu as pltpu
from jax.sharding import Mesh, PartitionSpec as P

epsilon = 1e-06
bf16 = jnp.bfloat16
f32 = jnp.float32
SEQ = ("z", "x")
TP = ("y", "c")
N_Z, N_X, N_Y, N_C = 16, 4, 4, 2
N_SEQ, N_TP = N_Z * N_X, N_Y * N_C
CAP = 8


def silu_slope(z):
    s = jax.nn.sigmoid(z)
    return s * (1.0 + z * (1.0 - s))


def dot(a, b, dims, precision=None):
    return lax.dot_general(a, b, (dims, ((), ())), precision=precision, preferred_element_type=f32)


def exchange(x, axis):
    return lax.all_to_all(x, axis, split_axis=0, concat_axis=0, tiled=True)


def copies(x, axis, count):
    return exchange(jnp.broadcast_to(x[None], (count,) + x.shape), axis)


def query_kernel(core_ref, own_ref, other_ref, w_own_ref, w_other_ref, out_ref):
    @pl.when(pl.program_id(0) == 0)
    def _():
        out_ref[...] = jnp.zeros_like(out_ref)

    out_ref[...] += jnp.dot(
        own_ref[0], w_own_ref[0], preferred_element_type=f32
    ) + jnp.dot(other_ref[0], w_other_ref[0], preferred_element_type=f32)


def query_matmul(core, own, other, weights):
    groups, tokens, width = own.shape
    cols = weights.shape[2]
    return pl.pallas_call(
        query_kernel,
        out_shape=jax.ShapeDtypeStruct((tokens, cols), f32),
        grid_spec=pltpu.PrefetchScalarGridSpec(
            num_scalar_prefetch=1,
            grid=(groups,),
            in_specs=[
                pl.BlockSpec((1, tokens, width), lambda i, core: (i, 0, 0)),
                pl.BlockSpec((1, tokens, width), lambda i, core: (i, 0, 0)),
                pl.BlockSpec((1, width, cols), lambda i, core: (2 * i + core[0], 0, 0)),
                pl.BlockSpec((1, width, cols), lambda i, core: (2 * i + 1 - core[0], 0, 0)),
            ],
            out_specs=pl.BlockSpec((tokens, cols), lambda i, core: (0, 0)),
        ),
    )(core, own, other, weights, weights)


def partial_kernel(core_ref, grad_ref, w_ref, out_ref):
    out_ref[0] = dot(grad_ref[...], w_ref[0], ((1,), (1,))).astype(out_ref.dtype)


def partial_matmul(core, grad, weights):
    tokens, cols = grad.shape
    width = weights.shape[1]
    groups = weights.shape[0] // 2
    return pl.pallas_call(
        partial_kernel,
        out_shape=jax.ShapeDtypeStruct((groups, tokens, width), bf16),
        grid_spec=pltpu.PrefetchScalarGridSpec(
            num_scalar_prefetch=1,
            grid=(groups,),
            in_specs=[
                pl.BlockSpec((tokens, cols), lambda i, core: (0, 0)),
                pl.BlockSpec((1, width, cols), lambda i, core: (2 * i + core[0], 0, 0)),
            ],
            out_specs=pl.BlockSpec((1, tokens, width), lambda i, core: (i, 0, 0)),
        ),
    )(core, grad, weights)


def swap_cores(x):
    return lax.ppermute(x, "c", [(0, 1), (1, 0)])


def body(
    latent,
    pose_rows,
    dest_device,
    dest_slot,
    w_section1,
    w_section2,
    w_section3,
    shift_mod,
    scale_mod,
    w_query,
    bias_query,
    gain_query,
    cotangent,
):
    tokens, width = latent.shape
    rows = pose_rows.shape[0]
    cols = w_query.shape[1]
    full_width = width * N_TP
    query_width = cols * N_TP
    slots = N_SEQ * CAP
    c = lax.axis_index("c")
    core = c.astype(jnp.int32).reshape(1)

    w_rows = lax.all_gather(w_query, "x", axis=0, tiled=True)

    owner = dest_device[:, 0]
    marks = owner[:, None] == jnp.arange(N_SEQ, dtype=jnp.int32)[None, :]
    earlier = jnp.arange(rows)[:, None] > jnp.arange(rows)[None, :]
    before = dot(earlier.astype(bf16), marks.astype(bf16), ((1,), (0,)))
    rank = jnp.sum(jnp.where(marks, before, 0.0), axis=1).astype(jnp.int32)
    position = owner * CAP + rank
    place = (jnp.arange(slots, dtype=jnp.int32)[:, None] == position[None, :]).astype(bf16)
    half = pose_rows.shape[1] // 2
    pose_half = lax.dynamic_slice_in_dim(pose_rows, c * half, half, axis=1)
    label = jnp.broadcast_to((dest_slot + 1).astype(bf16)[:, None], (rows, half))
    packed = dot(place, jnp.concatenate([pose_half, label], axis=1), ((1,), (0,))).astype(bf16)
    outgoing = jnp.concatenate(
        [packed[:, :half].reshape(N_SEQ, CAP, half), packed[:, half:].reshape(N_SEQ, CAP, half)],
        axis=1,
    )
    w_rows, outgoing = lax.optimization_barrier((w_rows, outgoing))
    weights = lax.all_gather(w_rows, "z", axis=0, tiled=True).reshape(N_TP, width, cols)
    incoming = exchange(outgoing, SEQ)
    pose = lax.all_gather(incoming[:, :CAP].reshape(slots, half), "c", axis=1, tiled=True)
    slot = incoming[:, CAP:, :1].reshape(slots, 1).astype(jnp.int32) - 1
    select = (slot == jnp.arange(tokens, dtype=jnp.int32)[None, :]).astype(bf16)

    cell_in, c_one = w_section1.shape
    c_two = w_section2.shape[1]
    in_cell = jnp.arange(16 * cell_in) // cell_in
    out_cell = jnp.arange(16 * c_one) // c_one
    big_i, big_j, a, b = out_cell // 8, (out_cell // 4) % 2, (out_cell // 2) % 2, out_cell % 2
    from_cell = 4 * (2 * big_i + a) + 2 * big_j + b
    cell_mask = in_cell[:, None] == from_cell[None, :]
    w_one = jnp.where(cell_mask, jnp.tile(w_section1, (16, 16)), jnp.zeros((), bf16))
    quad = jnp.arange(4 * c_two) // c_two
    w_two = jnp.where(
        quad[:, None] == quad[None, :], jnp.tile(w_section2, (4, 4)), jnp.zeros((), bf16)
    )
    z_one = dot(pose, w_one, ((1,), (0,)))
    stacked_one = jax.nn.silu(z_one).astype(bf16)
    z_two = dot(stacked_one, w_two, ((1,), (0,)))
    stacked_two = jax.nn.silu(z_two).astype(bf16)
    pose_tokens = dot(stacked_two, w_section3, ((1,), (0,))).astype(bf16)
    guidance = dot(select, pose_tokens, ((0,), (0,)))
    summed = latent.astype(f32) + guidance

    local_mean = jnp.mean(summed, axis=1)
    local_square = jnp.sum((summed - local_mean[:, None]) ** 2, axis=1)
    stats = copies(jnp.stack([local_mean, local_square]), TP, N_TP)
    center = jnp.mean(stats[:, 0], axis=0)
    spread = (
        jnp.sum(stats[:, 1], axis=0) + width * jnp.sum((stats[:, 0] - center) ** 2, axis=0)
    ) / full_width
    inverse = lax.rsqrt(spread + epsilon)[:, None]
    normed = (summed - center[:, None]) * inverse
    modulated = (normed * (1.0 + scale_mod) + shift_mod).astype(bf16)
    own = copies(modulated, "y", N_Y)
    other = swap_cores(own)

    query = query_matmul(core, own, other, weights) + bias_query
    upstream = cotangent.astype(f32) * gain_query
    sums = copies(
        jnp.stack([jnp.sum(query * query, axis=1), jnp.sum(upstream * query, axis=1)]), TP, N_TP
    )
    sums = jnp.sum(sums, axis=0)
    rinv = lax.rsqrt(sums[0] / query_width + epsilon)[:, None]
    along = (sums[1] / query_width)[:, None]
    normed_query = (query * rinv * gain_query).astype(bf16)
    query_grad = (upstream * rinv - query * along * rinv**3).astype(bf16)

    theirs = swap_cores(partial_matmul(1 - core, query_grad, weights))
    mine = partial_matmul(core, query_grad, weights)
    pair = (mine.astype(f32) + theirs.astype(f32)).astype(bf16)
    modulated_grad = jnp.sum(exchange(pair, "y").astype(f32), axis=0)
    normed_grad = modulated_grad * (1.0 + scale_mod)
    sums = copies(
        jnp.stack([jnp.sum(normed_grad, axis=1), jnp.sum(normed_grad * normed, axis=1)]), TP, N_TP
    )
    sums = jnp.sum(sums, axis=0) / full_width
    latent_grad = inverse * (normed_grad - sums[0][:, None] - normed * sums[1][:, None])
    latent_grad = latent_grad.astype(bf16)

    slot_grad = dot(select, latent_grad, ((1,), (0,))).astype(bf16)
    grad_three = dot(stacked_two, slot_grad, ((0,), (0,)))
    two_grad = dot(slot_grad, w_section3, ((1,), (1,))) * silu_slope(z_two)
    grad_two = sum(
        dot(
            stacked_one[:, k * c_two : (k + 1) * c_two].astype(f32),
            two_grad[:, k * c_two : (k + 1) * c_two],
            ((0,), (0,)),
            lax.Precision.HIGHEST,
        )
        for k in range(4)
    )
    one_grad = dot(
        two_grad, w_two.astype(f32), ((1,), (1,)), lax.Precision.HIGHEST
    ) * silu_slope(z_one)
    cross = dot(pose.astype(f32), one_grad, ((0,), (0,)), lax.Precision.HIGHEST)
    cross = jnp.where(cell_mask, cross, 0.0)
    cross = jnp.sum(cross.reshape(16, cell_in, 16 * c_one), axis=0)
    grad_one = sum(cross[:, k * c_one : (k + 1) * c_one] for k in range(16))

    per = grad_three.shape[0] // N_SEQ
    two_rows = c_two // N_SEQ
    small = jnp.concatenate(
        [
            grad_two.reshape(N_SEQ, two_rows, c_two),
            jnp.pad(
                grad_one.reshape(N_SEQ, 1, -1),
                ((0, 0), (0, 0), (0, c_two - grad_one.size // N_SEQ)),
            ),
            jnp.zeros((N_SEQ, per - two_rows - 1, c_two), f32),
        ],
        axis=1,
    )
    shares = jnp.concatenate([grad_three.reshape(N_SEQ, per, width), small], axis=2).astype(bf16)
    mine = jnp.sum(exchange(shares, SEQ).astype(f32), axis=0)
    section_three_grad = mine[:, :width]
    small = mine[: two_rows + 1, width:].reshape(1, (two_rows + 1) * c_two)
    small = jnp.sum(copies(small, TP, N_TP), axis=0)
    small = copies(small, SEQ, N_SEQ).reshape(N_SEQ, two_rows + 1, c_two)
    section_two_grad = small[:, :two_rows].reshape(grad_two.shape)
    section_one_grad = small[:, two_rows, : grad_one.size // N_SEQ].reshape(grad_one.shape)
    return (normed_query, section_three_grad, section_two_grad, section_one_grad)


def solution(mesh):
    fine = Mesh(mesh.devices.reshape(N_Z, N_X, N_Y, N_C), ("z", "x", "y", "c"))
    return jax.shard_map(
        body,
        mesh=fine,
        in_specs=(
            P(SEQ, TP),
            P(SEQ, None),
            P(SEQ, None),
            P(SEQ),
            P(),
            P(),
            P(None, TP),
            P(TP),
            P(TP),
            P(SEQ, TP),
            P(TP),
            P(TP),
            P(SEQ, TP),
        ),
        out_specs=(P(SEQ, TP), P(SEQ, TP), P(), P()),
        check_vma=False,
    )
```

```python
import jax
import jax.numpy as jnp
from jax import lax
from jax.experimental import pallas as pl
from jax.experimental.pallas import tpu as pltpu
from jax.sharding import Mesh, PartitionSpec as P

epsilon = 1e-06
bf16 = jnp.bfloat16
f32 = jnp.float32
SEQ = ("z", "x")
TP = ("y", "c")
PLANE = ("x", "y", "c")
N_Z, N_X, N_Y, N_C = 16, 4, 4, 2
N_SEQ, N_TP, N_PLANE = N_Z * N_X, N_Y * N_C, N_X * N_Y * N_C
CAP = 8


def silu_slope(z):
    s = jax.nn.sigmoid(z)
    return s * (1.0 + z * (1.0 - s))


def dot(a, b, dims, precision=None):
    return lax.dot_general(a, b, (dims, ((), ())), precision=precision, preferred_element_type=f32)


def exchange(x, axis):
    return lax.all_to_all(x, axis, split_axis=0, concat_axis=0, tiled=True)


def copies(x, axis, count):
    return exchange(jnp.broadcast_to(x[None], (count,) + x.shape), axis)


def query_kernel(core_ref, own_ref, other_ref, w_own_ref, w_other_ref, out_ref):
    @pl.when(pl.program_id(0) == 0)
    def _():
        out_ref[...] = jnp.zeros_like(out_ref)

    out_ref[...] += jnp.dot(
        own_ref[0], w_own_ref[0], preferred_element_type=f32
    ) + jnp.dot(other_ref[0], w_other_ref[0], preferred_element_type=f32)


def query_matmul(core, own, other, weights):
    groups, tokens, width = own.shape
    cols = weights.shape[2]
    return pl.pallas_call(
        query_kernel,
        out_shape=jax.ShapeDtypeStruct((tokens, cols), f32),
        grid_spec=pltpu.PrefetchScalarGridSpec(
            num_scalar_prefetch=1,
            grid=(groups,),
            in_specs=[
                pl.BlockSpec((1, tokens, width), lambda i, core: (i, 0, 0)),
                pl.BlockSpec((1, tokens, width), lambda i, core: (i, 0, 0)),
                pl.BlockSpec((1, width, cols), lambda i, core: (2 * i + core[0], 0, 0)),
                pl.BlockSpec((1, width, cols), lambda i, core: (2 * i + 1 - core[0], 0, 0)),
            ],
            out_specs=pl.BlockSpec((tokens, cols), lambda i, core: (0, 0)),
        ),
    )(core, own, other, weights, weights)


def partial_kernel(core_ref, grad_ref, w_ref, out_ref):
    out_ref[0] = dot(w_ref[0], grad_ref[...], ((1,), (1,))).astype(out_ref.dtype)


def partial_matmul(core, grad, weights):
    tokens, cols = grad.shape
    width = weights.shape[1]
    groups = weights.shape[0] // 2
    return pl.pallas_call(
        partial_kernel,
        out_shape=jax.ShapeDtypeStruct((groups, width, tokens), bf16),
        grid_spec=pltpu.PrefetchScalarGridSpec(
            num_scalar_prefetch=1,
            grid=(groups,),
            in_specs=[
                pl.BlockSpec((tokens, cols), lambda i, core: (0, 0)),
                pl.BlockSpec((1, width, cols), lambda i, core: (2 * i + core[0], 0, 0)),
            ],
            out_specs=pl.BlockSpec((1, width, tokens), lambda i, core: (i, 0, 0)),
        ),
    )(core, grad, weights)


def halves(x):
    high = lax.reduce_precision(x, 8, 7)
    return jnp.stack([high, x - high]).astype(bf16)


def swap_cores(x):
    return lax.ppermute(x, "c", [(0, 1), (1, 0)])


def body(
    latent,
    pose_rows,
    dest_device,
    dest_slot,
    w_section1,
    w_section2,
    w_section3,
    shift_mod,
    scale_mod,
    w_query,
    bias_query,
    gain_query,
    cotangent,
):
    tokens, width = latent.shape
    rows = pose_rows.shape[0]
    cols = w_query.shape[1]
    full_width = width * N_TP
    query_width = cols * N_TP
    slots = N_SEQ * CAP
    c = lax.axis_index("c")
    core = c.astype(jnp.int32).reshape(1)

    w_rows = lax.all_gather(w_query, "x", axis=0, tiled=True)
    w_rows, pose_rows, dest_device, dest_slot = lax.optimization_barrier(
        (w_rows, pose_rows, dest_device, dest_slot)
    )
    weights = lax.all_gather(w_rows, "z", axis=0, tiled=True).reshape(N_TP, width, cols)

    owner = dest_device[:, 0]
    marks = owner[:, None] == jnp.arange(N_SEQ, dtype=jnp.int32)[None, :]
    earlier = jnp.arange(rows)[:, None] > jnp.arange(rows)[None, :]
    before = dot(earlier.astype(bf16), marks.astype(bf16), ((1,), (0,)))
    rank = jnp.sum(jnp.where(marks, before, 0.0), axis=1).astype(jnp.int32)
    position = owner * CAP + rank
    place = (jnp.arange(slots, dtype=jnp.int32)[:, None] == position[None, :]).astype(bf16)
    half = pose_rows.shape[1] // 2
    pose_half = lax.dynamic_slice_in_dim(pose_rows, c * half, half, axis=1)
    label = jnp.broadcast_to((dest_slot + 1).astype(bf16)[:, None], (rows, half))
    packed = dot(place, jnp.concatenate([pose_half, label], axis=1), ((1,), (0,))).astype(bf16)
    outgoing = jnp.concatenate(
        [packed[:, :half].reshape(N_SEQ, CAP, half), packed[:, half:].reshape(N_SEQ, CAP, half)],
        axis=1,
    )
    incoming = exchange(outgoing, SEQ)
    pose = lax.all_gather(incoming[:, :CAP].reshape(slots, half), "c", axis=1, tiled=True)
    slot = incoming[:, CAP:, :1].reshape(slots, 1).astype(jnp.int32) - 1
    select = (slot == jnp.arange(tokens, dtype=jnp.int32)[None, :]).astype(bf16)

    cell_in, c_one = w_section1.shape
    c_two = w_section2.shape[1]
    in_cell = jnp.arange(16 * cell_in) // cell_in
    out_cell = jnp.arange(16 * c_one) // c_one
    big_i, big_j, a, b = out_cell // 8, (out_cell // 4) % 2, (out_cell // 2) % 2, out_cell % 2
    from_cell = 4 * (2 * big_i + a) + 2 * big_j + b
    cell_mask = in_cell[:, None] == from_cell[None, :]
    w_one = jnp.where(cell_mask, jnp.tile(w_section1, (16, 16)), jnp.zeros((), bf16))
    quad = jnp.arange(4 * c_two) // c_two
    w_two = jnp.where(
        quad[:, None] == quad[None, :], jnp.tile(w_section2, (4, 4)), jnp.zeros((), bf16)
    )
    z_one = dot(pose, w_one, ((1,), (0,)))
    stacked_one = jax.nn.silu(z_one).astype(bf16)
    z_two = dot(stacked_one, w_two, ((1,), (0,)))
    stacked_two = jax.nn.silu(z_two).astype(bf16)
    pose_tokens = dot(stacked_two, w_section3, ((1,), (0,))).astype(bf16)
    guidance = dot(select, pose_tokens, ((0,), (0,)))
    summed = latent.astype(f32) + guidance

    local_mean = jnp.mean(summed, axis=1)
    local_square = jnp.sum((summed - local_mean[:, None]) ** 2, axis=1)
    stats = copies(jnp.stack([local_mean, local_square]), TP, N_TP)
    center = jnp.mean(stats[:, 0], axis=0)
    spread = (
        jnp.sum(stats[:, 1], axis=0) + width * jnp.sum((stats[:, 0] - center) ** 2, axis=0)
    ) / full_width
    inverse = lax.rsqrt(spread + epsilon)[:, None]
    normed = (summed - center[:, None]) * inverse
    modulated = (normed * (1.0 + scale_mod) + shift_mod).astype(bf16)
    extra = jnp.concatenate([halves(1.0 + scale_mod), halves(shift_mod)])
    extra = jnp.pad(extra, ((0, 12), (0, 0)))
    own = copies(jnp.concatenate([modulated, extra]), "y", N_Y)
    other = swap_cores(own)
    normed_t, slope_one, slope_two, other = lax.optimization_barrier(
        (normed.T, silu_slope(z_one), silu_slope(z_two), other)
    )

    products = query_matmul(core, own, other, weights)
    query = products[:tokens] + bias_query
    scale_w = products[tokens] + products[tokens + 1]
    shift_w = products[tokens + 2] + products[tokens + 3] + bias_query
    upstream = cotangent.astype(f32) * gain_query
    sums = copies(
        jnp.stack(
            [
                jnp.sum(query * query, axis=1),
                jnp.sum(upstream * query, axis=1),
                jnp.sum(query * scale_w, axis=1),
                jnp.sum(upstream * scale_w, axis=1),
                jnp.sum(query * shift_w, axis=1),
                jnp.sum(upstream * shift_w, axis=1),
            ]
        ),
        TP,
        N_TP,
    )
    sums = jnp.sum(sums, axis=0)
    rinv = lax.rsqrt(sums[0] / query_width + epsilon)
    along = sums[1] / query_width
    pull = along * rinv**3
    grad_mean = (sums[3] * rinv - sums[2] * pull) / full_width
    grad_cross = ((sums[1] - sums[5]) * rinv - (sums[0] - sums[4]) * pull) / full_width
    rinv, pull = rinv[:, None], pull[:, None]
    normed_query = (query * rinv * gain_query).astype(bf16)
    query_grad = (upstream * rinv - query * pull).astype(bf16)

    theirs = swap_cores(partial_matmul(1 - core, query_grad, weights))
    mine = partial_matmul(core, query_grad, weights)
    pair = (mine.astype(f32) + theirs.astype(f32)).astype(bf16)
    modulated_grad = jnp.sum(exchange(pair, "y").astype(f32), axis=0)
    normed_grad = modulated_grad * (1.0 + scale_mod)[:, None]
    latent_grad = (
        inverse.reshape(1, tokens)
        * (normed_grad - grad_mean[None, :] - normed_t * grad_cross[None, :])
    ).astype(bf16)

    slot_grad = dot(select, latent_grad, ((1,), (1,))).astype(bf16)
    grad_three = dot(stacked_two, slot_grad, ((0,), (0,))).astype(bf16)
    per = grad_three.shape[0] // N_SEQ
    grad_three = grad_three.reshape(N_Z, N_X, per, width).transpose(1, 0, 2, 3)
    grad_three, slot_grad = lax.optimization_barrier((grad_three, slot_grad))
    grad_three = exchange(grad_three, "x")

    two_grad = dot(slot_grad, w_section3, ((1,), (1,))) * slope_two
    grad_two = sum(
        dot(
            stacked_one[:, k * c_two : (k + 1) * c_two].astype(f32),
            two_grad[:, k * c_two : (k + 1) * c_two],
            ((0,), (0,)),
            lax.Precision.HIGHEST,
        )
        for k in range(4)
    )
    one_grad = dot(two_grad, w_two.astype(f32), ((1,), (1,)), lax.Precision.HIGHEST) * slope_one
    cross = dot(pose.astype(f32), one_grad, ((0,), (0,)), lax.Precision.HIGHEST)
    cross = jnp.where(cell_mask, cross, 0.0)
    cross = jnp.sum(cross.reshape(16, cell_in, 16 * c_one), axis=0)
    grad_one = sum(cross[:, k * c_one : (k + 1) * c_one] for k in range(16))

    rows_two = c_two // N_PLANE
    left = grad_one.size // N_PLANE
    small = jnp.concatenate(
        [
            grad_two.reshape(N_PLANE, rows_two, c_two),
            jnp.pad(grad_one.reshape(N_PLANE, 1, left), ((0, 0), (0, 0), (0, c_two - left))),
        ],
        axis=1,
    )
    small, grad_three = lax.optimization_barrier((small, grad_three))
    small = jnp.sum(exchange(small, PLANE), axis=0)
    grad_three = jnp.sum(grad_three.astype(f32), axis=0).astype(bf16)
    small = jnp.broadcast_to(small.reshape(1, 1, width).astype(bf16), (N_Z, 1, width))
    total = exchange(jnp.concatenate([grad_three, small], axis=1), "z")
    total = jnp.sum(total.astype(f32), axis=0)
    section_three_grad = total[:per]
    small = copies(total[per:], PLANE, N_PLANE).reshape(N_PLANE, rows_two + 1, c_two)
    section_two_grad = small[:, :rows_two].reshape(grad_two.shape)
    section_one_grad = small[:, rows_two, :left].reshape(grad_one.shape)
    return (normed_query, section_three_grad, section_two_grad, section_one_grad)


def solution(mesh):
    fine = Mesh(mesh.devices.reshape(N_Z, N_X, N_Y, N_C), ("z", "x", "y", "c"))
    return jax.shard_map(
        body,
        mesh=fine,
        in_specs=(
            P(SEQ, TP),
            P(SEQ, None),
            P(SEQ, None),
            P(SEQ),
            P(),
            P(),
            P(None, TP),
            P(TP),
            P(TP),
            P(SEQ, TP),
            P(TP),
            P(TP),
            P(SEQ, TP),
        ),
        out_specs=(P(SEQ, TP), P(SEQ, TP), P(), P()),
        check_vma=False,
    )
```

```python
import jax
import jax.numpy as jnp
from jax import lax
from jax.experimental import pallas as pl
from jax.experimental.pallas import tpu as pltpu
from jax.sharding import Mesh, PartitionSpec as P

epsilon = 1e-06
bf16 = jnp.bfloat16
f32 = jnp.float32
SEQ = ("z", "x")
TP = ("y", "c")
N_Z, N_X, N_Y, N_C = 16, 4, 4, 2
N_SEQ, N_TP = N_Z * N_X, N_Y * N_C
CAP = 8


def silu_slope(z):
    s = jax.nn.sigmoid(z)
    return s * (1.0 + z * (1.0 - s))


def dot(a, b, dims, precision=None):
    return lax.dot_general(a, b, (dims, ((), ())), precision=precision, preferred_element_type=f32)


def exchange(x, axis):
    return lax.all_to_all(x, axis, split_axis=0, concat_axis=0, tiled=True)


def copies(x, axis, count):
    return exchange(jnp.broadcast_to(x[None], (count,) + x.shape), axis)


def query_kernel(core_ref, own_ref, other_ref, w_own_ref, w_other_ref, out_ref):
    @pl.when(pl.program_id(0) == 0)
    def _():
        out_ref[...] = jnp.zeros_like(out_ref)

    out_ref[...] += jnp.dot(
        own_ref[0], w_own_ref[0], preferred_element_type=f32
    ) + jnp.dot(other_ref[0], w_other_ref[0], preferred_element_type=f32)


def query_matmul(core, own, other, weights):
    groups, tokens, width = own.shape
    cols = weights.shape[2]
    return pl.pallas_call(
        query_kernel,
        out_shape=jax.ShapeDtypeStruct((tokens, cols), f32),
        grid_spec=pltpu.PrefetchScalarGridSpec(
            num_scalar_prefetch=1,
            grid=(groups,),
            in_specs=[
                pl.BlockSpec((1, tokens, width), lambda i, core: (i, 0, 0)),
                pl.BlockSpec((1, tokens, width), lambda i, core: (i, 0, 0)),
                pl.BlockSpec((1, width, cols), lambda i, core: (2 * i + core[0], 0, 0)),
                pl.BlockSpec((1, width, cols), lambda i, core: (2 * i + 1 - core[0], 0, 0)),
            ],
            out_specs=pl.BlockSpec((tokens, cols), lambda i, core: (0, 0)),
        ),
    )(core, own, other, weights, weights)


def partial_kernel(core_ref, grad_ref, w_ref, out_ref):
    out_ref[0] = dot(w_ref[0], grad_ref[...], ((1,), (1,))).astype(out_ref.dtype)


def partial_matmul(core, grad, weights):
    tokens, cols = grad.shape
    width = weights.shape[1]
    groups = weights.shape[0] // 2
    return pl.pallas_call(
        partial_kernel,
        out_shape=jax.ShapeDtypeStruct((groups, width, tokens), bf16),
        grid_spec=pltpu.PrefetchScalarGridSpec(
            num_scalar_prefetch=1,
            grid=(groups,),
            in_specs=[
                pl.BlockSpec((tokens, cols), lambda i, core: (0, 0)),
                pl.BlockSpec((1, width, cols), lambda i, core: (2 * i + core[0], 0, 0)),
            ],
            out_specs=pl.BlockSpec((1, width, tokens), lambda i, core: (i, 0, 0)),
        ),
    )(core, grad, weights)


def halves(x):
    high = lax.reduce_precision(x, 8, 7)
    return jnp.stack([high, x - high]).astype(bf16)


def swap_cores(x):
    return lax.ppermute(x, "c", [(0, 1), (1, 0)])


def body(
    latent,
    pose_rows,
    dest_device,
    dest_slot,
    w_section1,
    w_section2,
    w_section3,
    shift_mod,
    scale_mod,
    w_query,
    bias_query,
    gain_query,
    cotangent,
):
    tokens, width = latent.shape
    rows = pose_rows.shape[0]
    cols = w_query.shape[1]
    full_width = width * N_TP
    query_width = cols * N_TP
    slots = N_SEQ * CAP
    c = lax.axis_index("c")
    core = c.astype(jnp.int32).reshape(1)

    w_rows = copies(w_query, "x", N_X).reshape(N_X * w_query.shape[0], cols)
    w_rows, pose_rows, dest_device, dest_slot = lax.optimization_barrier(
        (w_rows, pose_rows, dest_device, dest_slot)
    )
    weights = lax.all_gather(w_rows, "z", axis=0, tiled=True).reshape(N_TP, width, cols)

    owner = dest_device[:, 0]
    marks = owner[:, None] == jnp.arange(N_SEQ, dtype=jnp.int32)[None, :]
    earlier = jnp.arange(rows)[:, None] > jnp.arange(rows)[None, :]
    before = dot(earlier.astype(bf16), marks.astype(bf16), ((1,), (0,)))
    rank = jnp.sum(jnp.where(marks, before, 0.0), axis=1).astype(jnp.int32)
    position = owner * CAP + rank
    place = (jnp.arange(slots, dtype=jnp.int32)[:, None] == position[None, :]).astype(bf16)
    half = pose_rows.shape[1] // 2
    pose_half = lax.dynamic_slice_in_dim(pose_rows, c * half, half, axis=1)
    label = jnp.broadcast_to((dest_slot + 1).astype(bf16)[:, None], (rows, half))
    packed = dot(place, jnp.concatenate([pose_half, label], axis=1), ((1,), (0,))).astype(bf16)
    outgoing = jnp.concatenate(
        [packed[:, :half].reshape(N_SEQ, CAP, half), packed[:, half:].reshape(N_SEQ, CAP, half)],
        axis=1,
    )
    incoming = exchange(outgoing, SEQ)
    pose = lax.all_gather(incoming[:, :CAP].reshape(slots, half), "c", axis=1, tiled=True)
    slot = incoming[:, CAP:, :1].reshape(slots, 1).astype(jnp.int32) - 1
    select = (slot == jnp.arange(tokens, dtype=jnp.int32)[None, :]).astype(bf16)

    cell_in, c_one = w_section1.shape
    c_two = w_section2.shape[1]
    in_cell = jnp.arange(16 * cell_in) // cell_in
    out_cell = jnp.arange(16 * c_one) // c_one
    big_i, big_j, a, b = out_cell // 8, (out_cell // 4) % 2, (out_cell // 2) % 2, out_cell % 2
    from_cell = 4 * (2 * big_i + a) + 2 * big_j + b
    cell_mask = in_cell[:, None] == from_cell[None, :]
    w_one = jnp.where(cell_mask, jnp.tile(w_section1, (16, 16)), jnp.zeros((), bf16))
    quad = jnp.arange(4 * c_two) // c_two
    w_two = jnp.where(
        quad[:, None] == quad[None, :], jnp.tile(w_section2, (4, 4)), jnp.zeros((), bf16)
    )
    z_one = dot(pose, w_one, ((1,), (0,)))
    stacked_one = jax.nn.silu(z_one).astype(bf16)
    z_two = dot(stacked_one, w_two, ((1,), (0,)))
    stacked_two = jax.nn.silu(z_two).astype(bf16)
    pose_tokens = dot(stacked_two, w_section3, ((1,), (0,))).astype(bf16)
    guidance = dot(select, pose_tokens, ((0,), (0,)))
    summed = latent.astype(f32) + guidance

    local_mean = jnp.mean(summed, axis=1)
    local_square = jnp.sum((summed - local_mean[:, None]) ** 2, axis=1)
    stats = copies(jnp.stack([local_mean, local_square]), TP, N_TP)
    center = jnp.mean(stats[:, 0], axis=0)
    spread = (
        jnp.sum(stats[:, 1], axis=0) + width * jnp.sum((stats[:, 0] - center) ** 2, axis=0)
    ) / full_width
    inverse = lax.rsqrt(spread + epsilon)[:, None]
    normed = (summed - center[:, None]) * inverse
    modulated = (normed * (1.0 + scale_mod) + shift_mod).astype(bf16)
    extra = jnp.concatenate([halves(1.0 + scale_mod), halves(shift_mod)])
    extra = jnp.pad(extra, ((0, 12), (0, 0)))
    own = copies(jnp.concatenate([modulated, extra]), "y", N_Y)
    other = swap_cores(own)
    normed_t, slope_one, slope_two, other = lax.optimization_barrier(
        (normed.T, silu_slope(z_one), silu_slope(z_two), other)
    )

    products = query_matmul(core, own, other, weights)
    query = products[:tokens] + bias_query
    scale_w = products[tokens] + products[tokens + 1]
    shift_w = products[tokens + 2] + products[tokens + 3] + bias_query
    upstream = cotangent.astype(f32) * gain_query
    sums = copies(
        jnp.stack(
            [
                jnp.sum(query * query, axis=1),
                jnp.sum(upstream * query, axis=1),
                jnp.sum(query * scale_w, axis=1),
                jnp.sum(upstream * scale_w, axis=1),
                jnp.sum(query * shift_w, axis=1),
                jnp.sum(upstream * shift_w, axis=1),
            ]
        ),
        TP,
        N_TP,
    )
    sums = jnp.sum(sums, axis=0)
    rinv = lax.rsqrt(sums[0] / query_width + epsilon)
    along = sums[1] / query_width
    pull = along * rinv**3
    grad_mean = (sums[3] * rinv - sums[2] * pull) / full_width
    grad_cross = ((sums[1] - sums[5]) * rinv - (sums[0] - sums[4]) * pull) / full_width
    rinv, pull = rinv[:, None], pull[:, None]
    normed_query = (query * rinv * gain_query).astype(bf16)
    query_grad = (upstream * rinv - query * pull).astype(bf16)

    theirs = swap_cores(partial_matmul(1 - core, query_grad, weights))
    mine = partial_matmul(core, query_grad, weights)
    pair = (mine.astype(f32) + theirs.astype(f32)).astype(bf16)
    modulated_grad = jnp.sum(exchange(pair, "y").astype(f32), axis=0)
    normed_grad = modulated_grad * (1.0 + scale_mod)[:, None]
    latent_grad = (
        inverse.reshape(1, tokens)
        * (normed_grad - grad_mean[None, :] - normed_t * grad_cross[None, :])
    ).astype(bf16)

    slot_grad = dot(select, latent_grad, ((1,), (1,))).astype(bf16)
    grad_three = dot(stacked_two, slot_grad, ((0,), (0,))).astype(bf16)
    per = grad_three.shape[0] // N_SEQ
    grad_three = grad_three.reshape(N_Z, N_X, per, width).transpose(1, 0, 2, 3)

    two_grad = dot(slot_grad, w_section3, ((1,), (1,))) * slope_two
    grad_two = sum(
        dot(
            stacked_one[:, k * c_two : (k + 1) * c_two].astype(f32),
            two_grad[:, k * c_two : (k + 1) * c_two],
            ((0,), (0,)),
            lax.Precision.HIGHEST,
        )
        for k in range(4)
    )
    one_grad = dot(two_grad, w_two.astype(f32), ((1,), (1,)), lax.Precision.HIGHEST) * slope_one
    cross = dot(pose.astype(f32), one_grad, ((0,), (0,)), lax.Precision.HIGHEST)
    cross = jnp.where(cell_mask, cross, 0.0)
    cross = jnp.sum(cross.reshape(16, cell_in, 16 * c_one), axis=0)
    grad_one = sum(cross[:, k * c_one : (k + 1) * c_one] for k in range(16))

    rows_two = c_two // N_TP
    left = grad_one.size // N_TP
    lines = 4
    small = jnp.concatenate(
        [
            grad_two.reshape(N_TP, rows_two, c_two),
            jnp.pad(grad_one.reshape(N_TP, 1, left), ((0, 0), (0, 3), (0, c_two - left))),
        ],
        axis=1,
    )
    small = jnp.sum(exchange(small, TP), axis=0).astype(bf16).reshape(1, lines, width)
    shares = jnp.concatenate(
        [
            grad_three.reshape(N_X, N_Z * per, width),
            jnp.broadcast_to(small, (N_X, lines, width)),
        ],
        axis=1,
    )
    shares = jnp.sum(exchange(shares, "x").astype(f32), axis=0).astype(bf16)
    shares = jnp.concatenate(
        [
            shares[: N_Z * per].reshape(N_Z, per, width),
            jnp.broadcast_to(shares[None, N_Z * per :], (N_Z, lines, width)),
        ],
        axis=1,
    )
    total = jnp.sum(exchange(shares, "z").astype(f32), axis=0)
    section_three_grad = total[:per]
    small = copies(total[per:].reshape(lines * width // c_two, c_two), TP, N_TP)
    section_two_grad = small[:, :rows_two].reshape(grad_two.shape)
    section_one_grad = small[:, rows_two, :left].reshape(grad_one.shape)
    return (normed_query, section_three_grad, section_two_grad, section_one_grad)


def solution(mesh):
    fine = Mesh(mesh.devices.reshape(N_Z, N_X, N_Y, N_C), ("z", "x", "y", "c"))
    return jax.shard_map(
        body,
        mesh=fine,
        in_specs=(
            P(SEQ, TP),
            P(SEQ, None),
            P(SEQ, None),
            P(SEQ),
            P(),
            P(),
            P(None, TP),
            P(TP),
            P(TP),
            P(SEQ, TP),
            P(TP),
            P(TP),
            P(SEQ, TP),
        ),
        out_specs=(P(SEQ, TP), P(SEQ, TP), P(), P()),
        check_vma=False,
    )
```

```python
import jax
import jax.numpy as jnp
from jax import lax
from jax.experimental import pallas as pl
from jax.experimental.pallas import tpu as pltpu
from jax.sharding import Mesh, PartitionSpec as P

epsilon = 1e-06
bf16 = jnp.bfloat16
f32 = jnp.float32
SEQ = ("z", "x")
TP = ("y", "c")
N_Z, N_X, N_Y, N_C = 16, 4, 4, 2
N_SEQ, N_TP = N_Z * N_X, N_Y * N_C
CAP = 8


def silu_slope(z):
    s = jax.nn.sigmoid(z)
    return s * (1.0 + z * (1.0 - s))


def dot(a, b, dims, precision=None):
    return lax.dot_general(a, b, (dims, ((), ())), precision=precision, preferred_element_type=f32)


def exchange(x, axis):
    return lax.all_to_all(x, axis, split_axis=0, concat_axis=0, tiled=True)


def copies(x, axis, count):
    return exchange(jnp.broadcast_to(x[None], (count,) + x.shape), axis)


VMEM_LIMIT = 32 * 1024 * 1024
QUERY_VMEM_LIMIT = 52 * 1024 * 1024


def in_vmem(count):
    return [pl.BlockSpec(memory_space=pltpu.VMEM)] * count


def across(column, width):
    block = jnp.transpose(jnp.broadcast_to(column, (128, column.shape[1])))
    return jnp.concatenate([block] * (width // 128), axis=1)


def query_kernel(
    bias_ref, gain_ref, cot_ref, own_ref, other_ref, w_ref, out_ref, sums_ref, left, held, sems
):
    core = lax.axis_index("c")
    groups, _, width = own_ref.shape
    tokens, cols = out_ref.shape
    fetches = []
    for i in range(groups):
        for k, (source, which) in enumerate(
            ((own_ref, 2 * i + core), (other_ref, 2 * i + 1 - core))
        ):
            place = 2 * i + k
            fetches.append(pltpu.make_async_copy(source.at[i], left.at[place], sems.at[0, place]))
            fetches.append(
                pltpu.make_async_copy(
                    w_ref.at[which], held.at[pl.ds(place * width, width)], sems.at[1, place]
                )
            )
    for fetch in fetches:
        fetch.start()
    total = None
    for i in range(groups):
        for fetch in fetches[4 * i : 4 * (i + 1)]:
            fetch.wait()
        both = jnp.concatenate([left[2 * i], left[2 * i + 1]], axis=1)
        term = jnp.dot(
            both, held[2 * i * width : 2 * (i + 1) * width], preferred_element_type=f32
        )
        total = term if total is None else total + term
    query = total[:tokens] + bias_ref[...]
    out_ref[...] = query
    scale_w = total[tokens : tokens + 1] + total[tokens + 1 : tokens + 2]
    shift_w = total[tokens + 2 : tokens + 3] + total[tokens + 3 : tokens + 4] + bias_ref[...]
    upstream = cot_ref[...].astype(f32) * gain_ref[...]
    terms = (
        query * query,
        upstream * query,
        query * scale_w,
        upstream * scale_w,
        query * shift_w,
        upstream * shift_w,
    )
    rows = []
    for term in terms:
        lanes = sum(term[:, k : k + 128] for k in range(0, cols, 128))
        rows.append(jnp.sum(jnp.transpose(lanes), axis=0, keepdims=True))
    rows.append(jnp.zeros((8 - len(rows), tokens), f32))
    sums_ref[...] = jnp.broadcast_to(jnp.concatenate(rows, axis=0)[None], sums_ref.shape)


def query_matmul(own, other, bias, gain, cotangent, weights):
    tokens, cols = cotangent.shape
    return pl.pallas_call(
        query_kernel,
        name="query",
        out_shape=(
            jax.ShapeDtypeStruct((tokens, cols), f32),
            jax.ShapeDtypeStruct((N_TP, 8, tokens), f32),
        ),
        in_specs=in_vmem(3) + [pl.BlockSpec(memory_space=pl.ANY)] * 3,
        out_specs=tuple(in_vmem(2)),
        scratch_shapes=[
            pltpu.VMEM((2 * own.shape[0],) + own.shape[1:], bf16),
            pltpu.VMEM((weights.shape[0] * weights.shape[1], cols), bf16),
            pltpu.SemaphoreType.DMA((2, weights.shape[0])),
        ],
        compiler_params=pltpu.CompilerParams(vmem_limit_bytes=QUERY_VMEM_LIMIT),
    )(bias[None], gain[None], cotangent, own, other, weights)


def fetch_blocks(w_ref, held, sems, core):
    fetches = [
        pltpu.make_async_copy(w_ref.at[2 * i + core], held.at[i], sems.at[i])
        for i in range(held.shape[0])
    ]
    for fetch in fetches:
        fetch.start()
    return fetches


def token_scales(sums_ref, query_width, width):
    sums = jnp.sum(sums_ref[...], axis=0)
    rinv = lax.rsqrt(sums[0:1] / query_width + epsilon)
    pull = sums[1:2] / query_width * rinv * rinv * rinv
    return across(rinv, width), across(pull, width)


def theirs_kernel(sums_ref, query_ref, gain_ref, cot_ref, w_ref, out_ref, grad_ref, held, sems):
    fetches = fetch_blocks(w_ref, held, sems, 1 - lax.axis_index("c"))
    cols = query_ref.shape[1]
    rinv, pull = token_scales(sums_ref, N_TP * cols, cols)
    upstream = cot_ref[...].astype(f32) * gain_ref[...]
    grad_ref[...] = (upstream * rinv - query_ref[...] * pull).astype(bf16)
    for i, fetch in enumerate(fetches):
        fetch.wait()
        out_ref[i] = dot(grad_ref[...], held[i], ((1,), (1,))).astype(bf16)


def mine_kernel(sums_ref, query_ref, gain_ref, grad_ref, w_ref, out_ref, normed_ref, held, sems):
    fetches = fetch_blocks(w_ref, held, sems, lax.axis_index("c"))
    cols = query_ref.shape[1]
    for i, fetch in enumerate(fetches):
        fetch.wait()
        out_ref[i] = dot(grad_ref[...], held[i], ((1,), (1,))).astype(bf16)
    rinv, _ = token_scales(sums_ref, N_TP * cols, cols)
    normed_ref[...] = (query_ref[...] * rinv * gain_ref[...]).astype(bf16)


def partial_matmul(kernel, name, sums, query, gain, last, weights):
    tokens, cols = query.shape
    groups, width = weights.shape[0] // 2, weights.shape[1]
    return pl.pallas_call(
        kernel,
        name=name,
        out_shape=(
            jax.ShapeDtypeStruct((groups, tokens, width), bf16),
            jax.ShapeDtypeStruct((tokens, cols), bf16),
        ),
        in_specs=in_vmem(4) + [pl.BlockSpec(memory_space=pl.ANY)],
        out_specs=tuple(in_vmem(2)),
        scratch_shapes=[
            pltpu.VMEM((groups, width, cols), bf16),
            pltpu.SemaphoreType.DMA((groups,)),
        ],
        compiler_params=pltpu.CompilerParams(vmem_limit_bytes=VMEM_LIMIT),
        cost_estimate=pl.CostEstimate(
            flops=2 * groups * tokens * cols * width,
            bytes_accessed=2 * groups * width * cols,
            transcendentals=0,
        ),
    )(sums, query, gain[None], last, weights)


def halves(x):
    high = lax.reduce_precision(x, 8, 7)
    return jnp.stack([high, x - high]).astype(bf16)


def swap_cores(x):
    return lax.ppermute(x, "c", [(0, 1), (1, 0)])


def body(
    latent,
    pose_rows,
    dest_device,
    dest_slot,
    w_section1,
    w_section2,
    w_section3,
    shift_mod,
    scale_mod,
    w_query,
    bias_query,
    gain_query,
    cotangent,
):
    tokens, width = latent.shape
    rows = pose_rows.shape[0]
    cols = w_query.shape[1]
    full_width = width * N_TP
    query_width = cols * N_TP
    slots = N_SEQ * CAP
    c = lax.axis_index("c")

    w_rows = copies(w_query, "x", N_X).reshape(N_X * w_query.shape[0], cols)
    w_rows, pose_rows, dest_device, dest_slot = lax.optimization_barrier(
        (w_rows, pose_rows, dest_device, dest_slot)
    )
    weights = lax.all_gather(w_rows, "z", axis=0, tiled=True).reshape(N_TP, width, cols)

    owner = dest_device[:, 0]
    marks = owner[:, None] == jnp.arange(N_SEQ, dtype=jnp.int32)[None, :]
    earlier = jnp.arange(rows)[:, None] > jnp.arange(rows)[None, :]
    before = dot(earlier.astype(bf16), marks.astype(bf16), ((1,), (0,)))
    rank = jnp.sum(jnp.where(marks, before, 0.0), axis=1).astype(jnp.int32)
    position = owner * CAP + rank
    place = (jnp.arange(slots, dtype=jnp.int32)[:, None] == position[None, :]).astype(bf16)
    half = pose_rows.shape[1] // 2
    pose_half = lax.dynamic_slice_in_dim(pose_rows, c * half, half, axis=1)
    label = jnp.broadcast_to((dest_slot + 1).astype(bf16)[:, None], (rows, half))
    packed = dot(place, jnp.concatenate([pose_half, label], axis=1), ((1,), (0,))).astype(bf16)
    outgoing = jnp.concatenate(
        [packed[:, :half].reshape(N_SEQ, CAP, half), packed[:, half:].reshape(N_SEQ, CAP, half)],
        axis=1,
    )
    incoming = exchange(outgoing, SEQ)
    pose = lax.all_gather(incoming[:, :CAP].reshape(slots, half), "c", axis=1, tiled=True)
    slot = incoming[:, CAP:, :1].reshape(slots, 1).astype(jnp.int32) - 1
    select = (slot == jnp.arange(tokens, dtype=jnp.int32)[None, :]).astype(bf16)

    cell_in, c_one = w_section1.shape
    c_two = w_section2.shape[1]
    in_cell = jnp.arange(16 * cell_in) // cell_in
    out_cell = jnp.arange(16 * c_one) // c_one
    big_i, big_j, a, b = out_cell // 8, (out_cell // 4) % 2, (out_cell // 2) % 2, out_cell % 2
    from_cell = 4 * (2 * big_i + a) + 2 * big_j + b
    cell_mask = in_cell[:, None] == from_cell[None, :]
    w_one = jnp.where(cell_mask, jnp.tile(w_section1, (16, 16)), jnp.zeros((), bf16))
    quad = jnp.arange(4 * c_two) // c_two
    w_two = jnp.where(
        quad[:, None] == quad[None, :], jnp.tile(w_section2, (4, 4)), jnp.zeros((), bf16)
    )
    z_one = dot(pose, w_one, ((1,), (0,)))
    stacked_one = jax.nn.silu(z_one).astype(bf16)
    z_two = dot(stacked_one, w_two, ((1,), (0,)))
    stacked_two = jax.nn.silu(z_two).astype(bf16)
    pose_tokens = dot(stacked_two, w_section3, ((1,), (0,))).astype(bf16)
    guidance = dot(select, pose_tokens, ((0,), (0,)))
    summed = latent.astype(f32) + guidance

    local_mean = jnp.mean(summed, axis=1)
    local_square = jnp.sum((summed - local_mean[:, None]) ** 2, axis=1)
    stats = copies(jnp.stack([local_mean, local_square]), TP, N_TP)
    center = jnp.mean(stats[:, 0], axis=0)
    spread = (
        jnp.sum(stats[:, 1], axis=0) + width * jnp.sum((stats[:, 0] - center) ** 2, axis=0)
    ) / full_width
    inverse = lax.rsqrt(spread + epsilon)[:, None]
    normed = (summed - center[:, None]) * inverse
    modulated = (normed * (1.0 + scale_mod) + shift_mod).astype(bf16)
    extra = jnp.concatenate([halves(1.0 + scale_mod), halves(shift_mod)])
    extra = jnp.pad(extra, ((0, 12), (0, 0)))
    own = copies(jnp.concatenate([modulated, extra]), "y", N_Y)
    other = swap_cores(own)
    normed, slope_one, slope_two, other = lax.optimization_barrier(
        (normed, silu_slope(z_one), silu_slope(z_two), other)
    )

    query, sums = query_matmul(own, other, bias_query, gain_query, cotangent, weights)
    sums = exchange(sums, TP)
    theirs, query_grad = partial_matmul(
        theirs_kernel, "theirs", sums, query, gain_query, cotangent, weights
    )
    theirs = swap_cores(theirs)
    mine, normed_query = partial_matmul(
        mine_kernel, "mine", sums, query, gain_query, query_grad, weights
    )
    sums = jnp.sum(sums, axis=0)
    rinv = lax.rsqrt(sums[0] / query_width + epsilon)
    pull = sums[1] / query_width * rinv**3
    grad_mean = ((sums[3] * rinv - sums[2] * pull) / full_width)[:, None]
    grad_cross = (((sums[1] - sums[5]) * rinv - (sums[0] - sums[4]) * pull) / full_width)[:, None]
    pair = (mine.astype(f32) + theirs.astype(f32)).astype(bf16)
    modulated_grad = jnp.sum(exchange(pair, "y").astype(f32), axis=0)
    normed_grad = modulated_grad * (1.0 + scale_mod)
    latent_grad = (inverse * (normed_grad - grad_mean - normed * grad_cross)).astype(bf16)

    slot_grad = dot(select, latent_grad, ((1,), (0,))).astype(bf16)
    grad_three = dot(stacked_two, slot_grad, ((0,), (0,))).astype(bf16)
    per = grad_three.shape[0] // N_SEQ
    grad_three = grad_three.reshape(N_Z, N_X, per, width).transpose(1, 0, 2, 3)

    two_grad = dot(slot_grad, w_section3, ((1,), (1,))) * slope_two
    grad_two = sum(
        dot(
            stacked_one[:, k * c_two : (k + 1) * c_two].astype(f32),
            two_grad[:, k * c_two : (k + 1) * c_two],
            ((0,), (0,)),
            lax.Precision.HIGHEST,
        )
        for k in range(4)
    )
    one_grad = dot(two_grad, w_two.astype(f32), ((1,), (1,)), lax.Precision.HIGHEST) * slope_one
    cross = dot(pose.astype(f32), one_grad, ((0,), (0,)), lax.Precision.HIGHEST)
    cross = jnp.where(cell_mask, cross, 0.0)
    cross = jnp.sum(cross.reshape(16, cell_in, 16 * c_one), axis=0)
    grad_one = sum(cross[:, k * c_one : (k + 1) * c_one] for k in range(16))

    rows_two = c_two // N_TP
    left = grad_one.size // N_TP
    lines = 4
    small = jnp.concatenate(
        [
            grad_two.reshape(N_TP, rows_two, c_two),
            jnp.pad(grad_one.reshape(N_TP, 1, left), ((0, 0), (0, 3), (0, c_two - left))),
        ],
        axis=1,
    )
    small = jnp.sum(exchange(small, TP), axis=0).astype(bf16).reshape(1, lines, width)
    shares = jnp.concatenate(
        [
            grad_three.reshape(N_X, N_Z * per, width),
            jnp.broadcast_to(small, (N_X, lines, width)),
        ],
        axis=1,
    )
    shares = jnp.sum(exchange(shares, "x").astype(f32), axis=0).astype(bf16)
    shares = jnp.concatenate(
        [
            shares[: N_Z * per].reshape(N_Z, per, width),
            jnp.broadcast_to(shares[None, N_Z * per :], (N_Z, lines, width)),
        ],
        axis=1,
    )
    total = jnp.sum(exchange(shares, "z").astype(f32), axis=0)
    section_three_grad = total[:per]
    small = copies(total[per:].reshape(lines * width // c_two, c_two), TP, N_TP)
    section_two_grad = small[:, :rows_two].reshape(grad_two.shape)
    section_one_grad = small[:, rows_two, :left].reshape(grad_one.shape)
    return (normed_query, section_three_grad, section_two_grad, section_one_grad)


def solution(mesh):
    fine = Mesh(mesh.devices.reshape(N_Z, N_X, N_Y, N_C), ("z", "x", "y", "c"))
    return jax.shard_map(
        body,
        mesh=fine,
        in_specs=(
            P(SEQ, TP),
            P(SEQ, None),
            P(SEQ, None),
            P(SEQ),
            P(),
            P(),
            P(None, TP),
            P(TP),
            P(TP),
            P(SEQ, TP),
            P(TP),
            P(TP),
            P(SEQ, TP),
        ),
        out_specs=(P(SEQ, TP), P(SEQ, TP), P(), P()),
        check_vma=False,
    )
```

```python
import jax
import jax.numpy as jnp
from jax import lax
from jax.experimental import pallas as pl
from jax.experimental.pallas import tpu as pltpu
from jax.sharding import Mesh, PartitionSpec as P

epsilon = 1e-06
bf16 = jnp.bfloat16
f32 = jnp.float32
SEQ = ("z", "x")
TP = ("y", "c")
N_Z, N_X, N_Y, N_C = 16, 4, 4, 2
N_SEQ, N_TP = N_Z * N_X, N_Y * N_C
CAP = 8


def silu_slope(z):
    s = jax.nn.sigmoid(z)
    return s * (1.0 + z * (1.0 - s))


def dot(a, b, dims, precision=None):
    return lax.dot_general(a, b, (dims, ((), ())), precision=precision, preferred_element_type=f32)


def exchange(x, axis):
    return lax.all_to_all(x, axis, split_axis=0, concat_axis=0, tiled=True)


def copies(x, axis, count):
    return exchange(jnp.broadcast_to(x[None], (count,) + x.shape), axis)


VMEM_LIMIT = 32 * 1024 * 1024
QUERY_VMEM_LIMIT = 52 * 1024 * 1024


def in_vmem(count):
    return [pl.BlockSpec(memory_space=pltpu.VMEM)] * count


def across(column, width):
    block = jnp.transpose(jnp.broadcast_to(column, (128, column.shape[1])))
    return jnp.concatenate([block] * (width // 128), axis=1)


def query_kernel(
    bias_ref, gain_ref, cot_ref, own_ref, other_ref, w_ref, out_ref, sums_ref, left, held, sems
):
    core = lax.axis_index("c")
    groups, _, width = own_ref.shape
    tokens, cols = out_ref.shape
    fetches = []
    for i in range(groups):
        for k, (source, which) in enumerate(
            ((own_ref, 2 * i + core), (other_ref, 2 * i + 1 - core))
        ):
            place = 2 * i + k
            fetches.append(pltpu.make_async_copy(source.at[i], left.at[place], sems.at[0, place]))
            fetches.append(
                pltpu.make_async_copy(
                    w_ref.at[which], held.at[pl.ds(place * width, width)], sems.at[1, place]
                )
            )
    for fetch in fetches:
        fetch.start()
    total = None
    for i in range(groups):
        for fetch in fetches[4 * i : 4 * (i + 1)]:
            fetch.wait()
        both = jnp.concatenate([left[2 * i], left[2 * i + 1]], axis=1)
        term = jnp.dot(
            both, held[2 * i * width : 2 * (i + 1) * width], preferred_element_type=f32
        )
        total = term if total is None else total + term
    query = total[:tokens] + bias_ref[...]
    out_ref[...] = query
    scale_w = total[tokens : tokens + 1] + total[tokens + 1 : tokens + 2]
    shift_w = total[tokens + 2 : tokens + 3] + total[tokens + 3 : tokens + 4] + bias_ref[...]
    upstream = cot_ref[...].astype(f32) * gain_ref[...]
    terms = (
        query * query,
        upstream * query,
        query * scale_w,
        upstream * scale_w,
        query * shift_w,
        upstream * shift_w,
    )
    rows = []
    for term in terms:
        lanes = sum(term[:, k : k + 128] for k in range(0, cols, 128))
        rows.append(jnp.sum(jnp.transpose(lanes), axis=0, keepdims=True))
    rows.append(jnp.zeros((8 - len(rows), tokens), f32))
    sums_ref[...] = jnp.broadcast_to(jnp.concatenate(rows, axis=0)[None], sums_ref.shape)


def query_matmul(own, other, bias, gain, cotangent, weights):
    tokens, cols = cotangent.shape
    return pl.pallas_call(
        query_kernel,
        name="query",
        out_shape=(
            jax.ShapeDtypeStruct((tokens, cols), f32),
            jax.ShapeDtypeStruct((N_TP, 8, tokens), f32),
        ),
        in_specs=in_vmem(3) + [pl.BlockSpec(memory_space=pl.ANY)] * 3,
        out_specs=tuple(in_vmem(2)),
        scratch_shapes=[
            pltpu.VMEM((2 * own.shape[0],) + own.shape[1:], bf16),
            pltpu.VMEM((weights.shape[0] * weights.shape[1], cols), bf16),
            pltpu.SemaphoreType.DMA((2, weights.shape[0])),
        ],
        compiler_params=pltpu.CompilerParams(vmem_limit_bytes=QUERY_VMEM_LIMIT),
    )(bias[None], gain[None], cotangent, own, other, weights)


def fetch_blocks(w_ref, held, sems, core):
    fetches = [
        pltpu.make_async_copy(w_ref.at[2 * i + core], held.at[i], sems.at[i])
        for i in range(held.shape[0])
    ]
    for fetch in fetches:
        fetch.start()
    return fetches


def token_scales(sums_ref, query_width, width):
    sums = jnp.sum(sums_ref[...], axis=0)
    rinv = lax.rsqrt(sums[0:1] / query_width + epsilon)
    pull = sums[1:2] / query_width * rinv * rinv * rinv
    return across(rinv, width), across(pull, width)


def theirs_kernel(sums_ref, query_ref, gain_ref, cot_ref, w_ref, out_ref, grad_ref, held, sems):
    fetches = fetch_blocks(w_ref, held, sems, 1 - lax.axis_index("c"))
    cols = query_ref.shape[1]
    rinv, pull = token_scales(sums_ref, N_TP * cols, cols)
    upstream = cot_ref[...].astype(f32) * gain_ref[...]
    grad_ref[...] = (upstream * rinv - query_ref[...] * pull).astype(bf16)
    for i, fetch in enumerate(fetches):
        fetch.wait()
        out_ref[i] = dot(grad_ref[...], held[i], ((1,), (1,))).astype(bf16)


def mine_kernel(sums_ref, query_ref, gain_ref, grad_ref, w_ref, out_ref, normed_ref, held, sems):
    fetches = fetch_blocks(w_ref, held, sems, lax.axis_index("c"))
    cols = query_ref.shape[1]
    for i, fetch in enumerate(fetches):
        fetch.wait()
        out_ref[i] = dot(grad_ref[...], held[i], ((1,), (1,))).astype(bf16)
    rinv, _ = token_scales(sums_ref, N_TP * cols, cols)
    normed_ref[...] = (query_ref[...] * rinv * gain_ref[...]).astype(bf16)


def partial_matmul(kernel, name, sums, query, gain, last, weights):
    tokens, cols = query.shape
    groups, width = weights.shape[0] // 2, weights.shape[1]
    return pl.pallas_call(
        kernel,
        name=name,
        out_shape=(
            jax.ShapeDtypeStruct((groups, tokens, width), bf16),
            jax.ShapeDtypeStruct((tokens, cols), bf16),
        ),
        in_specs=in_vmem(4) + [pl.BlockSpec(memory_space=pl.ANY)],
        out_specs=tuple(in_vmem(2)),
        scratch_shapes=[
            pltpu.VMEM((groups, width, cols), bf16),
            pltpu.SemaphoreType.DMA((groups,)),
        ],
        compiler_params=pltpu.CompilerParams(vmem_limit_bytes=VMEM_LIMIT),
        cost_estimate=pl.CostEstimate(
            flops=2 * groups * tokens * cols * width,
            bytes_accessed=2 * groups * width * cols,
            transcendentals=0,
        ),
    )(sums, query, gain[None], last, weights)


def split(x):
    high = x.astype(bf16)
    return high, (x - high.astype(f32)).astype(bf16)


def back_kernel(
    sums_ref,
    inverse_ref,
    scale_ref,
    normed_ref,
    select_ref,
    w_three_ref,
    slope_two_ref,
    one_t_ref,
    w_two_t_ref,
    slope_one_ref,
    pose_t_ref,
    pair_ref,
    slot_ref,
    small_ref,
):
    width = normed_ref.shape[1]
    full = N_TP * width
    sums = jnp.sum(sums_ref[...], axis=0)
    sums = [sums[k : k + 1] for k in range(6)]
    rinv = lax.rsqrt(sums[0] / full + epsilon)
    pull = sums[1] / full * rinv * rinv * rinv
    grad_mean = (sums[3] * rinv - sums[2] * pull) / full
    grad_cross = ((sums[1] - sums[5]) * rinv - (sums[0] - sums[4]) * pull) / full
    total = sum(pair_ref[k].astype(f32) for k in range(pair_ref.shape[0]))
    normed_grad = total * (1.0 + scale_ref[...])
    latent_grad = across(inverse_ref[...], width) * (
        normed_grad - across(grad_mean, width) - normed_ref[...] * across(grad_cross, width)
    )
    slot_grad = dot(select_ref[...], latent_grad.astype(bf16), ((1,), (0,))).astype(bf16)
    slot_ref[...] = slot_grad
    two_grad = dot(slot_grad, w_three_ref[...], ((1,), (1,))) * slope_two_ref[...]
    part = w_two_t_ref.shape[0]
    grad_two = jnp.zeros((part, part), f32)
    one_grad = []
    for k in range(two_grad.shape[1] // part):
        here = slice(k * part, (k + 1) * part)
        back_one = 0.0
        for piece in split(two_grad[:, here]):
            grad_two += jnp.dot(one_t_ref[here, :], piece, preferred_element_type=f32)
            back_one += jnp.dot(piece, w_two_t_ref[...], preferred_element_type=f32)
        one_grad.append(back_one * slope_one_ref[:, here])
    one_grad = jnp.concatenate(one_grad, axis=1)
    cross = sum(
        jnp.dot(pose_t_ref[...], piece, preferred_element_type=f32) for piece in split(one_grad)
    )
    cell = lax.broadcasted_iota(jnp.int32, cross.shape, 0) >> 4
    block = lax.broadcasted_iota(jnp.int32, cross.shape, 1) >> 5
    holds = (block & 8) + ((block & 2) << 1) + ((block & 4) >> 1) + (block & 1)
    cross = jnp.where(cell == holds, cross, 0.0)
    cross = sum(cross[16 * k : 16 * (k + 1)] for k in range(16))
    cross = sum(cross[:, 128 * k : 128 * (k + 1)] for k in range(4))
    cross = cross + pltpu.roll(cross, 64, 1)
    grad_one = cross + pltpu.roll(cross, 32, 1)
    rows_two, rows_one = part // N_TP, 16 // N_TP
    for k in range(N_TP):
        small_ref[k, :rows_two] = grad_two[k * rows_two : (k + 1) * rows_two]
        small_ref[k, rows_two:] = jnp.concatenate(
            [grad_one[k * rows_one : (k + 1) * rows_one], jnp.zeros((4 - rows_one, part), f32)]
        )


def back(*operands):
    normed, select, w_two_t = operands[3], operands[4], operands[8]
    part = w_two_t.shape[0]
    return pl.pallas_call(
        back_kernel,
        name="back",
        out_shape=(
            jax.ShapeDtypeStruct((select.shape[0], normed.shape[1]), bf16),
            jax.ShapeDtypeStruct((N_TP, part // N_TP + 4, part), f32),
        ),
        in_specs=in_vmem(len(operands)),
        out_specs=tuple(in_vmem(2)),
        compiler_params=pltpu.CompilerParams(vmem_limit_bytes=VMEM_LIMIT),
    )(*operands)


def halves(x):
    high = lax.reduce_precision(x, 8, 7)
    return jnp.stack([high, x - high]).astype(bf16)


def swap_cores(x):
    return lax.ppermute(x, "c", [(0, 1), (1, 0)])


def body(
    latent,
    pose_rows,
    dest_device,
    dest_slot,
    w_section1,
    w_section2,
    w_section3,
    shift_mod,
    scale_mod,
    w_query,
    bias_query,
    gain_query,
    cotangent,
):
    tokens, width = latent.shape
    rows = pose_rows.shape[0]
    cols = w_query.shape[1]
    full_width = width * N_TP
    query_width = cols * N_TP
    slots = N_SEQ * CAP

    w_rows = copies(w_query, "x", N_X).reshape(N_X * w_query.shape[0], cols)
    w_rows, pose_rows, dest_device, dest_slot = lax.optimization_barrier(
        (w_rows, pose_rows, dest_device, dest_slot)
    )
    weights = lax.all_gather(w_rows, "z", axis=0, tiled=True).reshape(N_TP, width, cols)

    owner = dest_device[:, 0]
    marks = owner[:, None] == jnp.arange(N_SEQ, dtype=jnp.int32)[None, :]
    earlier = jnp.arange(rows)[:, None] > jnp.arange(rows)[None, :]
    before = dot(earlier.astype(bf16), marks.astype(bf16), ((1,), (0,)))
    rank = jnp.sum(jnp.where(marks, before, 0.0), axis=1).astype(jnp.int32)
    share = pose_rows.shape[1] // N_TP
    lane = jnp.arange(4 * share, dtype=jnp.int32)
    side, column = lane // (2 * share), lane % (2 * share)
    mine = lax.axis_index("y") * N_C + lax.axis_index("c")
    pick = (jnp.arange(pose_rows.shape[1])[:, None] == mine * share + column) & (column < share)
    line_data = dot(pose_rows, pick.astype(bf16), ((1,), (0,)))
    line_data = jnp.where(column == share, (dest_slot + 1).astype(f32)[:, None], line_data)
    line_data = jnp.where(side == rank[:, None] // (CAP // 2), line_data, 0.0).astype(bf16)
    line = owner * (CAP // 2) + rank % (CAP // 2)
    lines = slots // 2
    place = (jnp.arange(lines, dtype=jnp.int32)[:, None] == line[None, :]).astype(bf16)
    outgoing = dot(place, line_data, ((1,), (0,))).astype(bf16)
    incoming = exchange(outgoing.reshape(N_SEQ, CAP // 2, 4 * share), SEQ)
    incoming = incoming.reshape(lines, 4 * share)
    pieces = copies(incoming, TP, N_TP).transpose(1, 0, 2).reshape(lines, N_TP * 4 * share)
    source = jnp.arange(N_TP * 4 * share, dtype=jnp.int32)
    origin, source = source // (4 * share), source % (4 * share)
    to = jnp.where(
        source % (2 * share) < share,
        source // (2 * share) * N_TP * share + origin * share + source % (2 * share),
        -1,
    )
    order = (to[:, None] == jnp.arange(2 * N_TP * share, dtype=jnp.int32)[None, :]).astype(bf16)
    pose = dot(pieces, order, ((1,), (0,))).astype(bf16)
    pose = jnp.concatenate([pose[:, : N_TP * share], pose[:, N_TP * share :]])
    slot = jnp.concatenate(
        [incoming[:, share : share + 1], incoming[:, 3 * share : 3 * share + 1]]
    ).astype(jnp.int32) - 1
    select = (slot == jnp.arange(tokens, dtype=jnp.int32)[None, :]).astype(bf16)

    cell_in, c_one = w_section1.shape
    c_two = w_section2.shape[1]
    in_cell = jnp.arange(16 * cell_in) // cell_in
    out_cell = jnp.arange(16 * c_one) // c_one
    big_i, big_j, a, b = out_cell // 8, (out_cell // 4) % 2, (out_cell // 2) % 2, out_cell % 2
    from_cell = 4 * (2 * big_i + a) + 2 * big_j + b
    cell_mask = in_cell[:, None] == from_cell[None, :]
    w_one = jnp.where(cell_mask, jnp.tile(w_section1, (16, 16)), jnp.zeros((), bf16))
    quad = jnp.arange(4 * c_two) // c_two
    w_two = jnp.where(
        quad[:, None] == quad[None, :], jnp.tile(w_section2, (4, 4)), jnp.zeros((), bf16)
    )
    z_one = dot(pose, w_one, ((1,), (0,)))
    stacked_one = jax.nn.silu(z_one).astype(bf16)
    z_two = dot(stacked_one, w_two, ((1,), (0,)))
    stacked_two = jax.nn.silu(z_two).astype(bf16)
    pose_tokens = dot(stacked_two, w_section3, ((1,), (0,))).astype(bf16)
    guidance = dot(select, pose_tokens, ((0,), (0,)))
    summed = latent.astype(f32) + guidance

    local_mean = jnp.mean(summed, axis=1)
    local_square = jnp.sum((summed - local_mean[:, None]) ** 2, axis=1)
    stats = copies(jnp.stack([local_mean, local_square]), TP, N_TP)
    center = jnp.mean(stats[:, 0], axis=0)
    spread = (
        jnp.sum(stats[:, 1], axis=0) + width * jnp.sum((stats[:, 0] - center) ** 2, axis=0)
    ) / full_width
    inverse = lax.rsqrt(spread + epsilon)[:, None]
    normed = (summed - center[:, None]) * inverse
    modulated = (normed * (1.0 + scale_mod) + shift_mod).astype(bf16)
    extra = jnp.concatenate([halves(1.0 + scale_mod), halves(shift_mod)])
    extra = jnp.pad(extra, ((0, 12), (0, 0)))
    own = copies(jnp.concatenate([modulated, extra]), "y", N_Y)
    other = swap_cores(own)
    per = stacked_two.shape[1] // N_SEQ
    row = jnp.arange(stacked_two.shape[1], dtype=jnp.int32)
    leaves = row // per % N_X * (N_Z * per) + row // (per * N_X) * per + row % per
    order = (leaves[:, None] == row[None, :]).astype(bf16)
    ready = (
        normed,
        inverse.reshape(1, tokens),
        select,
        dot(stacked_two, order, ((1,), (0,))).astype(bf16),
        silu_slope(z_two),
        stacked_one.T,
        silu_slope(z_one),
        pose.T,
        w_section2.T,
    )
    ready, other = lax.optimization_barrier((ready, other))
    normed, inverse, select, leaving_two, slope_two, one_t, slope_one, pose_t, w_two_t = ready

    query, sums = query_matmul(own, other, bias_query, gain_query, cotangent, weights)
    sums = exchange(sums, TP)
    theirs, query_grad = partial_matmul(
        theirs_kernel, "theirs", sums, query, gain_query, cotangent, weights
    )
    theirs = swap_cores(theirs)
    mine, normed_query = partial_matmul(
        mine_kernel, "mine", sums, query, gain_query, query_grad, weights
    )
    pair = (mine.astype(f32) + theirs.astype(f32)).astype(bf16)
    pair = exchange(pair, "y")
    slot_grad, small = back(
        sums,
        inverse,
        scale_mod[None],
        normed,
        select,
        w_section3,
        slope_two,
        one_t,
        w_two_t,
        slope_one,
        pose_t,
        pair,
    )
    grad_three = dot(leaving_two, slot_grad, ((0,), (0,))).astype(bf16)

    rows_two = c_two // N_TP
    lines = 4
    small = jnp.sum(exchange(small, TP), axis=0).astype(bf16).reshape(1, lines, width)
    shares = jnp.concatenate(
        [
            grad_three.reshape(N_X, N_Z * per, width),
            jnp.broadcast_to(small, (N_X, lines, width)),
        ],
        axis=1,
    )
    shares = jnp.sum(exchange(shares, "x").astype(f32), axis=0).astype(bf16)
    shares = jnp.concatenate(
        [
            shares[: N_Z * per].reshape(N_Z, per, width),
            jnp.broadcast_to(shares[None, N_Z * per :], (N_Z, lines, width)),
        ],
        axis=1,
    )
    total = jnp.sum(exchange(shares, "z").astype(f32), axis=0)
    section_three_grad = total[:per]
    small = copies(total[per:].reshape(lines * width // c_two, c_two), TP, N_TP)
    section_two_grad = small[:, :rows_two].reshape(c_two, c_two)
    section_one_grad = small[:, rows_two : rows_two + cell_in // N_TP, :c_one]
    section_one_grad = section_one_grad.reshape(cell_in, c_one)
    return (normed_query, section_three_grad, section_two_grad, section_one_grad)


def solution(mesh):
    fine = Mesh(mesh.devices.reshape(N_Z, N_X, N_Y, N_C), ("z", "x", "y", "c"))
    return jax.shard_map(
        body,
        mesh=fine,
        in_specs=(
            P(SEQ, TP),
            P(SEQ, None),
            P(SEQ, None),
            P(SEQ),
            P(),
            P(),
            P(None, TP),
            P(TP),
            P(TP),
            P(SEQ, TP),
            P(TP),
            P(TP),
            P(SEQ, TP),
        ),
        out_specs=(P(SEQ, TP), P(SEQ, TP), P(), P()),
        check_vma=False,
    )
```

```python
import jax
import jax.numpy as jnp
from jax import lax
from jax.experimental import pallas as pl
from jax.experimental.pallas import tpu as pltpu
from jax.sharding import Mesh, PartitionSpec as P

epsilon = 1e-06
bf16 = jnp.bfloat16
f32 = jnp.float32
SEQ = ("z", "x")
TP = ("y", "c")
N_Z, N_X, N_Y, N_C = 16, 4, 4, 2
N_SEQ, N_TP = N_Z * N_X, N_Y * N_C
CAP = 8


def silu_slope(z):
    s = jax.nn.sigmoid(z)
    return s * (1.0 + z * (1.0 - s))


def dot(a, b, dims, precision=None):
    return lax.dot_general(a, b, (dims, ((), ())), precision=precision, preferred_element_type=f32)


def exchange(x, axis):
    return lax.all_to_all(x, axis, split_axis=0, concat_axis=0, tiled=True)


def copies(x, axis, count):
    return exchange(jnp.broadcast_to(x[None], (count,) + x.shape), axis)


VMEM_LIMIT = 32 * 1024 * 1024
BACK_VMEM_LIMIT = 56 * 1024 * 1024
QUERY_VMEM_LIMIT = 52 * 1024 * 1024


def in_vmem(count):
    return [pl.BlockSpec(memory_space=pltpu.VMEM)] * count


def across(column, width):
    block = jnp.transpose(jnp.broadcast_to(column, (128, column.shape[1])))
    return jnp.concatenate([block] * (width // 128), axis=1)


def query_kernel(
    bias_ref, gain_ref, cot_ref, own_ref, other_ref, w_ref, out_ref, sums_ref, left, held, sems
):
    core = lax.axis_index("c")
    groups, _, width = own_ref.shape
    tokens, cols = out_ref.shape
    fetches = []
    for i in range(groups):
        for k, (source, which) in enumerate(
            ((own_ref, 2 * i + core), (other_ref, 2 * i + 1 - core))
        ):
            place = 2 * i + k
            fetches.append(pltpu.make_async_copy(source.at[i], left.at[place], sems.at[0, place]))
            fetches.append(
                pltpu.make_async_copy(
                    w_ref.at[which], held.at[pl.ds(place * width, width)], sems.at[1, place]
                )
            )
    for fetch in fetches:
        fetch.start()
    total = None
    for i in range(groups):
        for fetch in fetches[4 * i : 4 * (i + 1)]:
            fetch.wait()
        both = jnp.concatenate([left[2 * i], left[2 * i + 1]], axis=1)
        term = jnp.dot(
            both, held[2 * i * width : 2 * (i + 1) * width], preferred_element_type=f32
        )
        total = term if total is None else total + term
    query = total[:tokens] + bias_ref[...]
    out_ref[...] = query
    scale_w = total[tokens : tokens + 1] + total[tokens + 1 : tokens + 2]
    shift_w = total[tokens + 2 : tokens + 3] + total[tokens + 3 : tokens + 4] + bias_ref[...]
    upstream = cot_ref[...].astype(f32) * gain_ref[...]
    terms = (
        query * query,
        upstream * query,
        query * scale_w,
        upstream * scale_w,
        query * shift_w,
        upstream * shift_w,
    )
    rows = []
    for term in terms:
        lanes = sum(term[:, k : k + 128] for k in range(0, cols, 128))
        rows.append(jnp.sum(jnp.transpose(lanes), axis=0, keepdims=True))
    rows.append(jnp.zeros((8 - len(rows), tokens), f32))
    sums_ref[...] = jnp.broadcast_to(jnp.concatenate(rows, axis=0)[None], sums_ref.shape)


def query_matmul(own, other, bias, gain, cotangent, weights):
    tokens, cols = cotangent.shape
    return pl.pallas_call(
        query_kernel,
        name="query",
        out_shape=(
            jax.ShapeDtypeStruct((tokens, cols), f32),
            jax.ShapeDtypeStruct((N_TP, 8, tokens), f32),
        ),
        in_specs=in_vmem(3) + [pl.BlockSpec(memory_space=pl.ANY)] * 3,
        out_specs=tuple(in_vmem(2)),
        scratch_shapes=[
            pltpu.VMEM((2 * own.shape[0],) + own.shape[1:], bf16),
            pltpu.VMEM((weights.shape[0] * weights.shape[1], cols), bf16),
            pltpu.SemaphoreType.DMA((2, weights.shape[0])),
        ],
        compiler_params=pltpu.CompilerParams(vmem_limit_bytes=QUERY_VMEM_LIMIT),
    )(bias[None], gain[None], cotangent, own, other, weights)


def fetch_blocks(w_ref, held, sems, core):
    fetches = [
        pltpu.make_async_copy(w_ref.at[2 * i + core], held.at[i], sems.at[i])
        for i in range(held.shape[0])
    ]
    for fetch in fetches:
        fetch.start()
    return fetches


def token_scales(sums_ref, query_width, width):
    sums = jnp.sum(sums_ref[...], axis=0)
    rinv = lax.rsqrt(sums[0:1] / query_width + epsilon)
    pull = sums[1:2] / query_width * rinv * rinv * rinv
    return across(rinv, width), across(pull, width)


def theirs_kernel(sums_ref, query_ref, gain_ref, cot_ref, w_ref, out_ref, grad_ref, held, sems):
    fetches = fetch_blocks(w_ref, held, sems, 1 - lax.axis_index("c"))
    cols = query_ref.shape[1]
    rinv, pull = token_scales(sums_ref, N_TP * cols, cols)
    upstream = cot_ref[...].astype(f32) * gain_ref[...]
    grad_ref[...] = (upstream * rinv - query_ref[...] * pull).astype(bf16)
    for i, fetch in enumerate(fetches):
        fetch.wait()
        out_ref[i] = dot(grad_ref[...], held[i], ((1,), (1,))).astype(bf16)


def mine_kernel(sums_ref, query_ref, gain_ref, grad_ref, w_ref, out_ref, normed_ref, held, sems):
    fetches = fetch_blocks(w_ref, held, sems, lax.axis_index("c"))
    cols = query_ref.shape[1]
    for i, fetch in enumerate(fetches):
        fetch.wait()
        out_ref[i] = dot(grad_ref[...], held[i], ((1,), (1,))).astype(bf16)
    rinv, _ = token_scales(sums_ref, N_TP * cols, cols)
    normed_ref[...] = (query_ref[...] * rinv * gain_ref[...]).astype(bf16)


def partial_matmul(kernel, name, sums, query, gain, last, weights):
    tokens, cols = query.shape
    groups, width = weights.shape[0] // 2, weights.shape[1]
    return pl.pallas_call(
        kernel,
        name=name,
        out_shape=(
            jax.ShapeDtypeStruct((groups, tokens, width), bf16),
            jax.ShapeDtypeStruct((tokens, cols), bf16),
        ),
        in_specs=in_vmem(4) + [pl.BlockSpec(memory_space=pl.ANY)],
        out_specs=tuple(in_vmem(2)),
        scratch_shapes=[
            pltpu.VMEM((groups, width, cols), bf16),
            pltpu.SemaphoreType.DMA((groups,)),
        ],
        compiler_params=pltpu.CompilerParams(vmem_limit_bytes=VMEM_LIMIT),
        cost_estimate=pl.CostEstimate(
            flops=2 * groups * tokens * cols * width,
            bytes_accessed=2 * groups * width * cols,
            transcendentals=0,
        ),
    )(sums, query, gain[None], last, weights)


def split(x):
    high = x.astype(bf16)
    return high, (x - high.astype(f32)).astype(bf16)


def back_kernel(
    sums_ref,
    inverse_ref,
    scale_ref,
    w_two_t_ref,
    pair_hbm,
    normed_hbm,
    select_hbm,
    w_three_hbm,
    slope_two_hbm,
    one_t_hbm,
    slope_one_hbm,
    pose_t_hbm,
    slot_ref,
    small_ref,
    pair_ref,
    normed_ref,
    select_ref,
    w_three_ref,
    slope_two_ref,
    one_t_ref,
    slope_one_ref,
    pose_t_ref,
    sems,
):
    far = (
        pair_hbm,
        normed_hbm,
        select_hbm,
        w_three_hbm,
        slope_two_hbm,
        one_t_hbm,
        slope_one_hbm,
        pose_t_hbm,
    )
    near = (
        pair_ref,
        normed_ref,
        select_ref,
        w_three_ref,
        slope_two_ref,
        one_t_ref,
        slope_one_ref,
        pose_t_ref,
    )
    fetches = [
        pltpu.make_async_copy(source, target, sems.at[k])
        for k, (source, target) in enumerate(zip(far, near, strict=True))
    ]
    for fetch in fetches:
        fetch.start()
    width = normed_ref.shape[1]
    full = N_TP * width
    sums = jnp.sum(sums_ref[...], axis=0)
    sums = [sums[k : k + 1] for k in range(6)]
    rinv = lax.rsqrt(sums[0] / full + epsilon)
    pull = sums[1] / full * rinv * rinv * rinv
    grad_mean = (sums[3] * rinv - sums[2] * pull) / full
    grad_cross = ((sums[1] - sums[5]) * rinv - (sums[0] - sums[4]) * pull) / full
    for fetch in fetches[:3]:
        fetch.wait()
    total = sum(pair_ref[k].astype(f32) for k in range(pair_ref.shape[0]))
    normed_grad = total * (1.0 + scale_ref[...])
    latent_grad = across(inverse_ref[...], width) * (
        normed_grad - across(grad_mean, width) - normed_ref[...] * across(grad_cross, width)
    )
    slot_grad = dot(select_ref[...], latent_grad.astype(bf16), ((1,), (0,))).astype(bf16)
    slot_ref[...] = slot_grad
    for fetch in fetches[3:]:
        fetch.wait()
    two_grad = dot(slot_grad, w_three_ref[...], ((1,), (1,))) * slope_two_ref[...]
    part = w_two_t_ref.shape[0]
    grad_two = jnp.zeros((part, part), f32)
    one_grad = []
    for k in range(two_grad.shape[1] // part):
        here = slice(k * part, (k + 1) * part)
        back_one = 0.0
        for piece in split(two_grad[:, here]):
            grad_two += jnp.dot(one_t_ref[here, :], piece, preferred_element_type=f32)
            back_one += jnp.dot(piece, w_two_t_ref[...], preferred_element_type=f32)
        one_grad.append(back_one * slope_one_ref[:, here])
    one_grad = jnp.concatenate(one_grad, axis=1)
    cross = sum(
        jnp.dot(pose_t_ref[...], piece, preferred_element_type=f32) for piece in split(one_grad)
    )
    cell = lax.broadcasted_iota(jnp.int32, cross.shape, 0) >> 4
    block = lax.broadcasted_iota(jnp.int32, cross.shape, 1) >> 5
    holds = (block & 8) + ((block & 2) << 1) + ((block & 4) >> 1) + (block & 1)
    cross = jnp.where(cell == holds, cross, 0.0)
    cross = sum(cross[16 * k : 16 * (k + 1)] for k in range(16))
    cross = sum(cross[:, 128 * k : 128 * (k + 1)] for k in range(4))
    cross = cross + pltpu.roll(cross, 64, 1)
    grad_one = cross + pltpu.roll(cross, 32, 1)
    rows_two, rows_one = part // N_TP, 16 // N_TP
    for k in range(N_TP):
        small_ref[k, :rows_two] = grad_two[k * rows_two : (k + 1) * rows_two]
        small_ref[k, rows_two:] = jnp.concatenate(
            [grad_one[k * rows_one : (k + 1) * rows_one], jnp.zeros((8 - rows_one, part), f32)]
        )


def back(near, far):
    normed, select = far[1:3]
    part = near[3].shape[0]
    return pl.pallas_call(
        back_kernel,
        name="back",
        out_shape=(
            jax.ShapeDtypeStruct((select.shape[0], normed.shape[1]), bf16),
            jax.ShapeDtypeStruct((N_TP, part // N_TP + 8, part), f32),
        ),
        in_specs=in_vmem(len(near)) + [pl.BlockSpec(memory_space=pl.ANY)] * len(far),
        out_specs=tuple(in_vmem(2)),
        scratch_shapes=[pltpu.VMEM(x.shape, x.dtype) for x in far]
        + [pltpu.SemaphoreType.DMA((len(far),))],
        compiler_params=pltpu.CompilerParams(vmem_limit_bytes=BACK_VMEM_LIMIT),
    )(*near, *far)


def three_kernel(slot_ref, two_t_hbm, out_ref, two_t_ref, sem):
    fetch = pltpu.make_async_copy(two_t_hbm, two_t_ref, sem)
    fetch.start()
    fetch.wait()
    out_ref[...] = jnp.dot(
        two_t_ref[...], slot_ref[...], preferred_element_type=f32
    ).astype(out_ref.dtype)


def three(slot_grad, two_t):
    rows, slots = two_t.shape
    width = slot_grad.shape[1]
    return pl.pallas_call(
        three_kernel,
        name="three",
        out_shape=jax.ShapeDtypeStruct((rows, width), bf16),
        in_specs=in_vmem(1) + [pl.BlockSpec(memory_space=pl.ANY)],
        out_specs=pl.BlockSpec(memory_space=pltpu.VMEM),
        scratch_shapes=[pltpu.VMEM(two_t.shape, bf16), pltpu.SemaphoreType.DMA],
        compiler_params=pltpu.CompilerParams(vmem_limit_bytes=BACK_VMEM_LIMIT),
        cost_estimate=pl.CostEstimate(
            flops=2 * rows * slots * width, bytes_accessed=2 * rows * slots, transcendentals=0
        ),
    )(slot_grad, two_t)


def halves(x):
    high = lax.reduce_precision(x, 8, 7)
    return jnp.stack([high, x - high]).astype(bf16)


def swap_cores(x):
    return lax.ppermute(x, "c", [(0, 1), (1, 0)])


def body(
    latent,
    pose_rows,
    dest_device,
    dest_slot,
    w_section1,
    w_section2,
    w_section3,
    shift_mod,
    scale_mod,
    w_query,
    bias_query,
    gain_query,
    cotangent,
):
    tokens, width = latent.shape
    rows = pose_rows.shape[0]
    cols = w_query.shape[1]
    full_width = width * N_TP
    query_width = cols * N_TP
    slots = N_SEQ * CAP

    w_rows = copies(w_query, "x", N_X).reshape(N_X * w_query.shape[0], cols)
    w_rows, pose_rows, dest_device, dest_slot = lax.optimization_barrier(
        (w_rows, pose_rows, dest_device, dest_slot)
    )
    weights = lax.all_gather(w_rows, "z", axis=0, tiled=True).reshape(N_TP, width, cols)

    owner = dest_device[:, 0]
    marks = owner[:, None] == jnp.arange(N_SEQ, dtype=jnp.int32)[None, :]
    earlier = jnp.arange(rows)[:, None] > jnp.arange(rows)[None, :]
    before = dot(earlier.astype(bf16), marks.astype(bf16), ((1,), (0,)))
    rank = jnp.sum(jnp.where(marks, before, 0.0), axis=1).astype(jnp.int32)
    share = pose_rows.shape[1] // N_TP
    lane = jnp.arange(4 * share, dtype=jnp.int32)
    side, column = lane // (2 * share), lane % (2 * share)
    mine = lax.axis_index("y") * N_C + lax.axis_index("c")
    pick = (jnp.arange(pose_rows.shape[1])[:, None] == mine * share + column) & (column < share)
    line_data = dot(pose_rows, pick.astype(bf16), ((1,), (0,)))
    line_data = jnp.where(column == share, (dest_slot + 1).astype(f32)[:, None], line_data)
    line_data = jnp.where(side == rank[:, None] // (CAP // 2), line_data, 0.0).astype(bf16)
    line = owner * (CAP // 2) + rank % (CAP // 2)
    lines = slots // 2
    place = (jnp.arange(lines, dtype=jnp.int32)[:, None] == line[None, :]).astype(bf16)
    outgoing = dot(place, line_data, ((1,), (0,))).astype(bf16)
    incoming = exchange(outgoing.reshape(N_SEQ, CAP // 2, 4 * share), SEQ)
    incoming = incoming.reshape(lines, 4 * share)
    pieces = copies(incoming, TP, N_TP).transpose(1, 0, 2).reshape(lines, N_TP * 4 * share)
    source = jnp.arange(N_TP * 4 * share, dtype=jnp.int32)
    origin, source = source // (4 * share), source % (4 * share)
    to = jnp.where(
        source % (2 * share) < share,
        source // (2 * share) * N_TP * share + origin * share + source % (2 * share),
        -1,
    )
    order = (to[:, None] == jnp.arange(2 * N_TP * share, dtype=jnp.int32)[None, :]).astype(bf16)
    pose = dot(pieces, order, ((1,), (0,))).astype(bf16)
    pose = jnp.concatenate([pose[:, : N_TP * share], pose[:, N_TP * share :]])
    slot = jnp.concatenate(
        [incoming[:, share : share + 1], incoming[:, 3 * share : 3 * share + 1]]
    ).astype(jnp.int32) - 1
    select = (slot == jnp.arange(tokens, dtype=jnp.int32)[None, :]).astype(bf16)

    cell_in, c_one = w_section1.shape
    c_two = w_section2.shape[1]
    in_cell = jnp.arange(16 * cell_in) // cell_in
    out_cell = jnp.arange(16 * c_one) // c_one
    big_i, big_j, a, b = out_cell // 8, (out_cell // 4) % 2, (out_cell // 2) % 2, out_cell % 2
    from_cell = 4 * (2 * big_i + a) + 2 * big_j + b
    cell_mask = in_cell[:, None] == from_cell[None, :]
    w_one = jnp.where(cell_mask, jnp.tile(w_section1, (16, 16)), jnp.zeros((), bf16))
    quad = jnp.arange(4 * c_two) // c_two
    w_two = jnp.where(
        quad[:, None] == quad[None, :], jnp.tile(w_section2, (4, 4)), jnp.zeros((), bf16)
    )
    z_one = dot(pose, w_one, ((1,), (0,)))
    stacked_one = jax.nn.silu(z_one).astype(bf16)
    z_two = dot(stacked_one, w_two, ((1,), (0,)))
    stacked_two = jax.nn.silu(z_two).astype(bf16)
    pose_tokens = dot(stacked_two, w_section3, ((1,), (0,))).astype(bf16)
    guidance = dot(select, pose_tokens, ((0,), (0,)))
    summed = latent.astype(f32) + guidance

    local_mean = jnp.mean(summed, axis=1)
    local_square = jnp.sum((summed - local_mean[:, None]) ** 2, axis=1)
    stats = copies(jnp.stack([local_mean, local_square]), TP, N_TP)
    center = jnp.mean(stats[:, 0], axis=0)
    spread = (
        jnp.sum(stats[:, 1], axis=0) + width * jnp.sum((stats[:, 0] - center) ** 2, axis=0)
    ) / full_width
    inverse = lax.rsqrt(spread + epsilon)[:, None]
    normed = (summed - center[:, None]) * inverse
    modulated = (normed * (1.0 + scale_mod) + shift_mod).astype(bf16)
    extra = jnp.concatenate([halves(1.0 + scale_mod), halves(shift_mod)])
    extra = jnp.pad(extra, ((0, 12), (0, 0)))
    own = copies(jnp.concatenate([modulated, extra]), "y", N_Y)
    per = stacked_two.shape[1] // N_SEQ
    row = jnp.arange(stacked_two.shape[1], dtype=jnp.int32)
    leaves = row // per % N_X * (N_Z * per) + row // (per * N_X) * per + row % per
    order = (leaves[:, None] == row[None, :]).astype(bf16)
    ready = (
        normed,
        inverse.reshape(1, tokens),
        select,
        dot(order, stacked_two, ((0,), (1,))).astype(bf16),
        silu_slope(z_two),
        stacked_one.T,
        silu_slope(z_one),
        pose.T,
        w_section2.T,
    )
    ready, own = lax.optimization_barrier((ready, own))
    normed, inverse, select, leaving_two, slope_two, one_t, slope_one, pose_t, w_two_t = ready
    other = swap_cores(own)

    query, sums = query_matmul(own, other, bias_query, gain_query, cotangent, weights)
    sums = exchange(sums, TP)
    theirs, query_grad = partial_matmul(
        theirs_kernel, "theirs", sums, query, gain_query, cotangent, weights
    )
    theirs = swap_cores(theirs)
    mine, normed_query = partial_matmul(
        mine_kernel, "mine", sums, query, gain_query, query_grad, weights
    )
    pair = (mine.astype(f32) + theirs.astype(f32)).astype(bf16)
    pair = exchange(pair, "y")
    slot_grad, small = back(
        (sums, inverse, scale_mod[None], w_two_t),
        (pair, normed, select, w_section3, slope_two, one_t, slope_one, pose_t),
    )
    grad_three = three(slot_grad, leaving_two)

    rows_two = c_two // N_TP
    small = jnp.sum(exchange(small, TP), axis=0).astype(bf16)
    wide = small.shape[0] // per * c_two
    small = jnp.concatenate([small[k : k + per] for k in range(0, small.shape[0], per)], axis=1)
    small = jnp.pad(small, ((0, 0), (0, width - wide)))
    shares = jnp.concatenate(
        [
            grad_three.reshape(N_X, N_Z * per, width),
            jnp.broadcast_to(small[None], (N_X, per, width)),
        ],
        axis=1,
    )
    shares = jnp.sum(exchange(shares, "x").astype(f32), axis=0).astype(bf16)
    shares = jnp.concatenate(
        [
            shares[: N_Z * per].reshape(N_Z, per, width),
            jnp.broadcast_to(shares[None, N_Z * per :, :wide], (N_Z, per, wide)),
        ],
        axis=2,
    )
    total = jnp.sum(exchange(shares, "z").astype(f32), axis=0)
    section_three_grad = total[:, :width]
    small = [total[:, k : k + c_two] for k in range(width, width + wide, c_two)]
    small = copies(jnp.concatenate(small), TP, N_TP)
    section_two_grad = small[:, :rows_two].reshape(c_two, c_two)
    section_one_grad = small[:, rows_two : rows_two + cell_in // N_TP, :c_one]
    section_one_grad = section_one_grad.reshape(cell_in, c_one)
    return (normed_query, section_three_grad, section_two_grad, section_one_grad)


def solution(mesh):
    fine = Mesh(mesh.devices.reshape(N_Z, N_X, N_Y, N_C), ("z", "x", "y", "c"))
    return jax.shard_map(
        body,
        mesh=fine,
        in_specs=(
            P(SEQ, TP),
            P(SEQ, None),
            P(SEQ, None),
            P(SEQ),
            P(),
            P(),
            P(None, TP),
            P(TP),
            P(TP),
            P(SEQ, TP),
            P(TP),
            P(TP),
            P(SEQ, TP),
        ),
        out_specs=(P(SEQ, TP), P(SEQ, TP), P(), P()),
        check_vma=False,
    )
```

```python
import jax
import jax.numpy as jnp
from jax import lax
from jax.experimental import pallas as pl
from jax.experimental.pallas import tpu as pltpu
from jax.sharding import Mesh, PartitionSpec as P

epsilon = 1e-06
bf16 = jnp.bfloat16
f32 = jnp.float32
SEQ = ("z", "x")
TP = ("y", "c")
N_Z, N_X, N_Y, N_C = 16, 4, 4, 2
N_SEQ, N_TP = N_Z * N_X, N_Y * N_C
CAP = 8


def silu_slope(z):
    s = jax.nn.sigmoid(z)
    return s * (1.0 + z * (1.0 - s))


def dot(a, b, dims, precision=None):
    return lax.dot_general(a, b, (dims, ((), ())), precision=precision, preferred_element_type=f32)


def exchange(x, axis):
    return lax.all_to_all(x, axis, split_axis=0, concat_axis=0, tiled=True)


def copies(x, axis, count):
    return exchange(jnp.broadcast_to(x[None], (count,) + x.shape), axis)


VMEM_LIMIT = 24 * 1024 * 1024


def in_vmem(count):
    return [pl.BlockSpec(memory_space=pltpu.VMEM)] * count


def in_hbm(*arrays):
    return tuple(pltpu.with_memory_space_constraint(x, pltpu.HBM) for x in arrays)


def across(column, width):
    block = jnp.transpose(jnp.broadcast_to(column, (128, column.shape[1])))
    return jnp.concatenate([block] * (width // 128), axis=1)


def query_kernel(
    cot_ref,
    bias_hbm,
    gain_hbm,
    own_ref,
    other_ref,
    w_ref,
    out_ref,
    sums_ref,
    bias_ref,
    gain_ref,
    left,
    held,
    row_sems,
    sems,
):
    core = lax.axis_index("c")
    row_fetches = (
        pltpu.make_async_copy(bias_hbm, bias_ref, row_sems.at[0]),
        pltpu.make_async_copy(gain_hbm, gain_ref, row_sems.at[1]),
    )
    groups, _, width = own_ref.shape
    tokens, cols = out_ref.shape
    fetches = []
    for i in range(groups):
        for k, (source, which) in enumerate(
            ((own_ref, 2 * i + core), (other_ref, 2 * i + 1 - core))
        ):
            place = 2 * i + k
            fetches.append(pltpu.make_async_copy(source.at[i], left.at[place], sems.at[0, place]))
            fetches.append(
                pltpu.make_async_copy(
                    w_ref.at[which], held.at[pl.ds(place * width, width)], sems.at[1, place]
                )
            )
    for fetch in (*fetches, *row_fetches):
        fetch.start()
    total = None
    for i in range(groups):
        for fetch in fetches[4 * i : 4 * (i + 1)]:
            fetch.wait()
        both = jnp.concatenate([left[2 * i], left[2 * i + 1]], axis=1)
        term = jnp.dot(
            both, held[2 * i * width : 2 * (i + 1) * width], preferred_element_type=f32
        )
        total = term if total is None else total + term
    for fetch in row_fetches:
        fetch.wait()
    query = total[:tokens] + bias_ref[...]
    out_ref[...] = query
    scale_w = total[tokens : tokens + 1] + total[tokens + 1 : tokens + 2]
    shift_w = total[tokens + 2 : tokens + 3] + total[tokens + 3 : tokens + 4] + bias_ref[...]
    upstream = cot_ref[...].astype(f32) * gain_ref[...]
    terms = (
        query * query,
        upstream * query,
        query * scale_w,
        upstream * scale_w,
        query * shift_w,
        upstream * shift_w,
    )
    rows = []
    for term in terms:
        lanes = sum(term[:, k : k + 128] for k in range(0, cols, 128))
        rows.append(jnp.sum(jnp.transpose(lanes), axis=0, keepdims=True))
    rows.append(jnp.zeros((8 - len(rows), tokens), f32))
    sums_ref[...] = jnp.broadcast_to(jnp.concatenate(rows, axis=0)[None], sums_ref.shape)


def query_matmul(own, other, bias, gain, cotangent, weights):
    tokens, cols = cotangent.shape
    return pl.pallas_call(
        query_kernel,
        name="query",
        out_shape=(
            jax.ShapeDtypeStruct((tokens, cols), f32),
            jax.ShapeDtypeStruct((N_TP, 8, tokens), f32),
        ),
        in_specs=in_vmem(1) + [pl.BlockSpec(memory_space=pl.ANY)] * 5,
        out_specs=tuple(in_vmem(2)),
        scratch_shapes=[
            pltpu.VMEM((1, cols), f32),
            pltpu.VMEM((1, cols), f32),
            pltpu.VMEM((2 * own.shape[0],) + own.shape[1:], bf16),
            pltpu.VMEM((weights.shape[0] * weights.shape[1], cols), bf16),
            pltpu.SemaphoreType.DMA((2,)),
            pltpu.SemaphoreType.DMA((2, weights.shape[0])),
        ],
        compiler_params=pltpu.CompilerParams(vmem_limit_bytes=VMEM_LIMIT),
    )(cotangent, *in_hbm(bias[None], gain[None], own, other, weights))


def fetch_blocks(w_ref, held, sems, core):
    fetches = [
        pltpu.make_async_copy(w_ref.at[2 * i + core], held.at[i], sems.at[i])
        for i in range(held.shape[0])
    ]
    for fetch in fetches:
        fetch.start()
    return fetches


def token_scales(sums_ref, query_width, width):
    sums = jnp.sum(sums_ref[...], axis=0)
    rinv = lax.rsqrt(sums[0:1] / query_width + epsilon)
    pull = sums[1:2] / query_width * rinv * rinv * rinv
    return across(rinv, width), across(pull, width)


def theirs_kernel(sums_ref, query_ref, gain_ref, cot_ref, w_ref, out_ref, grad_ref, held, sems):
    fetches = fetch_blocks(w_ref, held, sems, 1 - lax.axis_index("c"))
    cols = query_ref.shape[1]
    rinv, pull = token_scales(sums_ref, N_TP * cols, cols)
    upstream = cot_ref[...].astype(f32) * gain_ref[...]
    grad_ref[...] = (upstream * rinv - query_ref[...] * pull).astype(bf16)
    for i, fetch in enumerate(fetches):
        fetch.wait()
        out_ref[i] = dot(grad_ref[...], held[i], ((1,), (1,))).astype(bf16)


def mine_kernel(sums_ref, query_ref, gain_ref, grad_ref, w_ref, out_ref, normed_ref, held, sems):
    fetches = fetch_blocks(w_ref, held, sems, lax.axis_index("c"))
    cols = query_ref.shape[1]
    for i, fetch in enumerate(fetches):
        fetch.wait()
        out_ref[i] = dot(grad_ref[...], held[i], ((1,), (1,))).astype(bf16)
    rinv, _ = token_scales(sums_ref, N_TP * cols, cols)
    normed_ref[...] = (query_ref[...] * rinv * gain_ref[...]).astype(bf16)


def partial_matmul(kernel, name, sums, query, gain, last, weights):
    tokens, cols = query.shape
    groups, width = weights.shape[0] // 2, weights.shape[1]
    return pl.pallas_call(
        kernel,
        name=name,
        out_shape=(
            jax.ShapeDtypeStruct((groups, tokens, width), bf16),
            jax.ShapeDtypeStruct((tokens, cols), bf16),
        ),
        in_specs=in_vmem(4) + [pl.BlockSpec(memory_space=pl.ANY)],
        out_specs=tuple(in_vmem(2)),
        scratch_shapes=[
            pltpu.VMEM((groups, width, cols), bf16),
            pltpu.SemaphoreType.DMA((groups,)),
        ],
        compiler_params=pltpu.CompilerParams(vmem_limit_bytes=VMEM_LIMIT),
        cost_estimate=pl.CostEstimate(
            flops=2 * groups * tokens * cols * width,
            bytes_accessed=2 * groups * width * cols,
            transcendentals=0,
        ),
    )(sums, query, gain[None], last, weights)


def split(x):
    high = x.astype(bf16)
    return high, (x - high.astype(f32)).astype(bf16)


def back_kernel(
    sums_ref,
    inverse_ref,
    scale_ref,
    w_two_t_ref,
    pair_ref,
    normed_ref,
    select_ref,
    one_t_ref,
    pose_t_ref,
    w_three_hbm,
    slope_two_hbm,
    slope_one_hbm,
    slot_hbm,
    small_ref,
    w_three_ref,
    slope_two_ref,
    slope_one_ref,
    slot_ref,
    sems,
):
    far = (w_three_hbm, slope_two_hbm, slope_one_hbm)
    near = (w_three_ref, slope_two_ref, slope_one_ref)
    fetches = [
        pltpu.make_async_copy(source, target, sems.at[k])
        for k, (source, target) in enumerate(zip(far, near, strict=True))
    ]
    for fetch in fetches:
        fetch.start()
    width = normed_ref.shape[1]
    full = N_TP * width
    sums = jnp.sum(sums_ref[...], axis=0)
    sums = [sums[k : k + 1] for k in range(6)]
    rinv = lax.rsqrt(sums[0] / full + epsilon)
    pull = sums[1] / full * rinv * rinv * rinv
    grad_mean = (sums[3] * rinv - sums[2] * pull) / full
    grad_cross = ((sums[1] - sums[5]) * rinv - (sums[0] - sums[4]) * pull) / full
    total = sum(pair_ref[k].astype(f32) for k in range(pair_ref.shape[0]))
    normed_grad = total * (1.0 + scale_ref[...])
    latent_grad = across(inverse_ref[...], width) * (
        normed_grad - across(grad_mean, width) - normed_ref[...] * across(grad_cross, width)
    )
    slot_grad = dot(select_ref[...], latent_grad.astype(bf16), ((1,), (0,))).astype(bf16)
    slot_ref[...] = slot_grad
    store = pltpu.make_async_copy(slot_ref, slot_hbm, sems.at[len(fetches)])
    store.start()
    for fetch in fetches:
        fetch.wait()
    two_grad = dot(slot_grad, w_three_ref[...], ((1,), (1,))) * slope_two_ref[...]
    part = w_two_t_ref.shape[0]
    grad_two = jnp.zeros((part, part), f32)
    one_grad = []
    for k in range(two_grad.shape[1] // part):
        here = slice(k * part, (k + 1) * part)
        back_one = 0.0
        for piece in split(two_grad[:, here]):
            grad_two += jnp.dot(one_t_ref[here, :], piece, preferred_element_type=f32)
            back_one += jnp.dot(piece, w_two_t_ref[...], preferred_element_type=f32)
        one_grad.append(back_one * slope_one_ref[:, here])
    one_grad = jnp.concatenate(one_grad, axis=1)
    cross = sum(
        jnp.dot(pose_t_ref[...], piece, preferred_element_type=f32) for piece in split(one_grad)
    )
    cell = lax.broadcasted_iota(jnp.int32, cross.shape, 0) >> 4
    block = lax.broadcasted_iota(jnp.int32, cross.shape, 1) >> 5
    holds = (block & 8) + ((block & 2) << 1) + ((block & 4) >> 1) + (block & 1)
    cross = jnp.where(cell == holds, cross, 0.0)
    cross = sum(cross[16 * k : 16 * (k + 1)] for k in range(16))
    cross = sum(cross[:, 128 * k : 128 * (k + 1)] for k in range(4))
    cross = cross + pltpu.roll(cross, 64, 1)
    grad_one = cross + pltpu.roll(cross, 32, 1)
    rows_two, rows_one = part // N_TP, 16 // N_TP
    for k in range(N_TP):
        small_ref[k, :rows_two] = grad_two[k * rows_two : (k + 1) * rows_two]
        small_ref[k, rows_two:] = jnp.concatenate(
            [grad_one[k * rows_one : (k + 1) * rows_one], jnp.zeros((8 - rows_one, part), f32)]
        )
    store.wait()


def back(near, far):
    normed, select = near[5:7]
    part = near[3].shape[0]
    return pl.pallas_call(
        back_kernel,
        name="back",
        out_shape=(
            pltpu.HBM((select.shape[0], normed.shape[1]), bf16),
            jax.ShapeDtypeStruct((N_TP, part // N_TP + 8, part), f32),
        ),
        in_specs=in_vmem(len(near)) + [pl.BlockSpec(memory_space=pl.ANY)] * len(far),
        out_specs=(pl.BlockSpec(memory_space=pltpu.HBM), *in_vmem(1)),
        scratch_shapes=[pltpu.VMEM(x.shape, x.dtype) for x in far]
        + [
            pltpu.VMEM((select.shape[0], normed.shape[1]), bf16),
            pltpu.SemaphoreType.DMA((len(far) + 1,)),
        ],
        compiler_params=pltpu.CompilerParams(vmem_limit_bytes=VMEM_LIMIT),
    )(*near, *in_hbm(*far))


def three_kernel(slot_hbm, two_t_hbm, out_ref, slot_ref, two_t_ref, sems):
    fetches = (
        pltpu.make_async_copy(slot_hbm, slot_ref, sems.at[0]),
        pltpu.make_async_copy(two_t_hbm, two_t_ref, sems.at[1]),
    )
    for fetch in fetches:
        fetch.start()
    for fetch in fetches:
        fetch.wait()
    out_ref[...] = jnp.dot(
        two_t_ref[...], slot_ref[...], preferred_element_type=f32
    ).astype(out_ref.dtype)


def three(slot_grad, two_t):
    rows, slots = two_t.shape
    width = slot_grad.shape[1]
    return pl.pallas_call(
        three_kernel,
        name="three",
        out_shape=jax.ShapeDtypeStruct((rows, width), bf16),
        in_specs=[pl.BlockSpec(memory_space=pl.ANY)] * 2,
        out_specs=pl.BlockSpec(memory_space=pltpu.VMEM),
        scratch_shapes=[
            pltpu.VMEM(slot_grad.shape, bf16),
            pltpu.VMEM(two_t.shape, bf16),
            pltpu.SemaphoreType.DMA((2,)),
        ],
        compiler_params=pltpu.CompilerParams(vmem_limit_bytes=VMEM_LIMIT),
        cost_estimate=pl.CostEstimate(
            flops=2 * rows * slots * width, bytes_accessed=2 * rows * slots, transcendentals=0
        ),
    )(*in_hbm(slot_grad, two_t))


def halves(x):
    high = lax.reduce_precision(x, 8, 7)
    return jnp.stack([high, x - high]).astype(bf16)


def swap_cores(x):
    return lax.ppermute(x, "c", [(0, 1), (1, 0)])


def body(
    latent,
    pose_rows,
    dest_device,
    dest_slot,
    w_section1,
    w_section2,
    w_section3,
    shift_mod,
    scale_mod,
    w_query,
    bias_query,
    gain_query,
    cotangent,
):
    tokens, width = latent.shape
    rows = pose_rows.shape[0]
    cols = w_query.shape[1]
    full_width = width * N_TP
    query_width = cols * N_TP
    slots = N_SEQ * CAP

    w_rows = copies(w_query, "x", N_X).reshape(N_X * w_query.shape[0], cols)
    w_rows, pose_rows, dest_device, dest_slot = lax.optimization_barrier(
        (w_rows, pose_rows, dest_device, dest_slot)
    )
    weights = lax.all_gather(w_rows, "z", axis=0, tiled=True).reshape(N_TP, width, cols)

    owner = dest_device[:, 0]
    marks = owner[:, None] == jnp.arange(N_SEQ, dtype=jnp.int32)[None, :]
    earlier = jnp.arange(rows)[:, None] > jnp.arange(rows)[None, :]
    before = dot(earlier.astype(bf16), marks.astype(bf16), ((1,), (0,)))
    rank = jnp.sum(jnp.where(marks, before, 0.0), axis=1).astype(jnp.int32)
    share = pose_rows.shape[1] // N_TP
    lane = jnp.arange(4 * share, dtype=jnp.int32)
    side, column = lane // (2 * share), lane % (2 * share)
    mine = lax.axis_index("y") * N_C + lax.axis_index("c")
    pick = (jnp.arange(pose_rows.shape[1])[:, None] == mine * share + column) & (column < share)
    line_data = dot(pose_rows, pick.astype(bf16), ((1,), (0,)))
    line_data = jnp.where(column == share, (dest_slot + 1).astype(f32)[:, None], line_data)
    line_data = jnp.where(side == rank[:, None] // (CAP // 2), line_data, 0.0).astype(bf16)
    line = owner * (CAP // 2) + rank % (CAP // 2)
    lines = slots // 2
    place = (jnp.arange(lines, dtype=jnp.int32)[:, None] == line[None, :]).astype(bf16)
    outgoing = dot(place, line_data, ((1,), (0,))).astype(bf16)
    incoming = exchange(outgoing.reshape(N_SEQ, CAP // 2, 4 * share), SEQ)
    incoming = incoming.reshape(lines, 4 * share)
    pieces = copies(incoming, TP, N_TP).transpose(1, 0, 2).reshape(lines, N_TP * 4 * share)
    source = jnp.arange(N_TP * 4 * share, dtype=jnp.int32)
    origin, source = source // (4 * share), source % (4 * share)
    to = jnp.where(
        source % (2 * share) < share,
        source // (2 * share) * N_TP * share + origin * share + source % (2 * share),
        -1,
    )
    order = (to[:, None] == jnp.arange(2 * N_TP * share, dtype=jnp.int32)[None, :]).astype(bf16)
    pose = dot(pieces, order, ((1,), (0,))).astype(bf16)
    pose = jnp.concatenate([pose[:, : N_TP * share], pose[:, N_TP * share :]])
    slot = jnp.concatenate(
        [incoming[:, share : share + 1], incoming[:, 3 * share : 3 * share + 1]]
    ).astype(jnp.int32) - 1
    select = (slot == jnp.arange(tokens, dtype=jnp.int32)[None, :]).astype(bf16)

    cell_in, c_one = w_section1.shape
    c_two = w_section2.shape[1]
    in_cell = jnp.arange(16 * cell_in) // cell_in
    out_cell = jnp.arange(16 * c_one) // c_one
    big_i, big_j, a, b = out_cell // 8, (out_cell // 4) % 2, (out_cell // 2) % 2, out_cell % 2
    from_cell = 4 * (2 * big_i + a) + 2 * big_j + b
    cell_mask = in_cell[:, None] == from_cell[None, :]
    w_one = jnp.where(cell_mask, jnp.tile(w_section1, (16, 16)), jnp.zeros((), bf16))
    quad = jnp.arange(4 * c_two) // c_two
    w_two = jnp.where(
        quad[:, None] == quad[None, :], jnp.tile(w_section2, (4, 4)), jnp.zeros((), bf16)
    )
    z_one = dot(pose, w_one, ((1,), (0,)))
    stacked_one = jax.nn.silu(z_one).astype(bf16)
    z_two = dot(stacked_one, w_two, ((1,), (0,)))
    stacked_two = jax.nn.silu(z_two).astype(bf16)
    pose_tokens = dot(stacked_two, w_section3, ((1,), (0,))).astype(bf16)
    guidance = dot(select, pose_tokens, ((0,), (0,)))
    summed = latent.astype(f32) + guidance

    local_mean = jnp.mean(summed, axis=1)
    local_square = jnp.sum((summed - local_mean[:, None]) ** 2, axis=1)
    stats = copies(jnp.stack([local_mean, local_square]), TP, N_TP)
    center = jnp.mean(stats[:, 0], axis=0)
    spread = (
        jnp.sum(stats[:, 1], axis=0) + width * jnp.sum((stats[:, 0] - center) ** 2, axis=0)
    ) / full_width
    inverse = lax.rsqrt(spread + epsilon)[:, None]
    normed = (summed - center[:, None]) * inverse
    modulated = (normed * (1.0 + scale_mod) + shift_mod).astype(bf16)
    extra = jnp.concatenate([halves(1.0 + scale_mod), halves(shift_mod)])
    extra = jnp.pad(extra, ((0, 12), (0, 0)))
    own = copies(jnp.concatenate([modulated, extra]), "y", N_Y)
    per = stacked_two.shape[1] // N_SEQ
    row = jnp.arange(stacked_two.shape[1], dtype=jnp.int32)
    leaves = row // per % N_X * (N_Z * per) + row // (per * N_X) * per + row % per
    order = (leaves[:, None] == row[None, :]).astype(bf16)
    ready = (
        normed,
        inverse.reshape(1, tokens),
        select,
        dot(order, stacked_two, ((0,), (1,))).astype(bf16),
        silu_slope(z_two),
        stacked_one.T,
        silu_slope(z_one),
        pose.T,
        w_section2.T,
    )
    ready, own = lax.optimization_barrier((ready, own))
    normed, inverse, select, leaving_two, slope_two, one_t, slope_one, pose_t, w_two_t = ready
    other = swap_cores(own)

    query, sums = query_matmul(own, other, bias_query, gain_query, cotangent, weights)
    sums = exchange(sums, TP)
    theirs, query_grad = partial_matmul(
        theirs_kernel, "theirs", sums, query, gain_query, cotangent, weights
    )
    theirs = swap_cores(theirs)
    mine, normed_query = partial_matmul(
        mine_kernel, "mine", sums, query, gain_query, query_grad, weights
    )
    pair = (mine.astype(f32) + theirs.astype(f32)).astype(bf16)
    pair = exchange(pair, "y")
    slot_grad, small = back(
        (sums, inverse, scale_mod[None], w_two_t, pair, normed, select, one_t, pose_t),
        (w_section3, slope_two, slope_one),
    )
    grad_three = three(slot_grad, leaving_two)

    rows_two = c_two // N_TP
    small = jnp.sum(exchange(small, TP), axis=0).astype(bf16)
    wide = small.shape[0] // per * c_two
    small = jnp.concatenate([small[k : k + per] for k in range(0, small.shape[0], per)], axis=1)
    small = jnp.pad(small, ((0, 0), (0, width - wide)))
    shares = jnp.concatenate(
        [
            grad_three.reshape(N_X, N_Z * per, width),
            jnp.broadcast_to(small[None], (N_X, per, width)),
        ],
        axis=1,
    )
    shares = jnp.sum(exchange(shares, "x").astype(f32), axis=0).astype(bf16)
    shares = jnp.concatenate(
        [
            shares[: N_Z * per].reshape(N_Z, per, width),
            jnp.broadcast_to(shares[None, N_Z * per :, :wide], (N_Z, per, wide)),
        ],
        axis=2,
    )
    total = jnp.sum(exchange(shares, "z").astype(f32), axis=0)
    section_three_grad = total[:, :width]
    small = [total[:, k : k + c_two] for k in range(width, width + wide, c_two)]
    small = copies(jnp.concatenate(small), TP, N_TP)
    section_two_grad = small[:, :rows_two].reshape(c_two, c_two)
    section_one_grad = small[:, rows_two : rows_two + cell_in // N_TP, :c_one]
    section_one_grad = section_one_grad.reshape(cell_in, c_one)
    return (normed_query, section_three_grad, section_two_grad, section_one_grad)


def solution(mesh):
    fine = Mesh(mesh.devices.reshape(N_Z, N_X, N_Y, N_C), ("z", "x", "y", "c"))
    return jax.shard_map(
        body,
        mesh=fine,
        in_specs=(
            P(SEQ, TP),
            P(SEQ, None),
            P(SEQ, None),
            P(SEQ),
            P(),
            P(),
            P(None, TP),
            P(TP),
            P(TP),
            P(SEQ, TP),
            P(TP),
            P(TP),
            P(SEQ, TP),
        ),
        out_specs=(P(SEQ, TP), P(SEQ, TP), P(), P()),
        check_vma=False,
    )
```

```python
import jax
import jax.numpy as jnp
from jax import lax
from jax.experimental import pallas as pl
from jax.experimental.pallas import tpu as pltpu
from jax.sharding import Mesh, PartitionSpec as P

epsilon = 1e-06
bf16 = jnp.bfloat16
f32 = jnp.float32
SEQ = ("z", "x")
TP = ("y", "c")
N_Z, N_X, N_Y, N_C = 16, 4, 4, 2
N_SEQ, N_TP = N_Z * N_X, N_Y * N_C
CAP = 8


def silu_slope(z):
    s = jax.nn.sigmoid(z)
    return s * (1.0 + z * (1.0 - s))


def dot(a, b, dims, precision=None):
    return lax.dot_general(a, b, (dims, ((), ())), precision=precision, preferred_element_type=f32)


def exchange(x, axis):
    return lax.all_to_all(x, axis, split_axis=0, concat_axis=0, tiled=True)


def copies(x, axis, count):
    return exchange(jnp.broadcast_to(x[None], (count,) + x.shape), axis)


VMEM_LIMIT = 24 * 1024 * 1024


def in_vmem(count):
    return [pl.BlockSpec(memory_space=pltpu.VMEM)] * count


def in_hbm(*arrays):
    return tuple(pltpu.with_memory_space_constraint(x, pltpu.HBM) for x in arrays)


def across(column, width):
    block = jnp.transpose(jnp.broadcast_to(column, (128, column.shape[1])))
    return jnp.concatenate([block] * (width // 128), axis=1)


def query_kernel(
    cot_ref,
    bias_hbm,
    gain_hbm,
    own_ref,
    other_ref,
    w_ref,
    out_ref,
    sums_ref,
    bias_ref,
    gain_ref,
    left,
    held,
    row_sems,
    sems,
):
    core = lax.axis_index("c")
    row_fetches = (
        pltpu.make_async_copy(bias_hbm, bias_ref, row_sems.at[0]),
        pltpu.make_async_copy(gain_hbm, gain_ref, row_sems.at[1]),
    )
    groups, _, width = own_ref.shape
    tokens, cols = out_ref.shape
    fetches = []
    for i in range(groups):
        for k, (source, which) in enumerate(
            ((own_ref, 2 * i + core), (other_ref, 2 * i + 1 - core))
        ):
            place = 2 * i + k
            fetches.append(pltpu.make_async_copy(source.at[i], left.at[place], sems.at[0, place]))
            fetches.append(
                pltpu.make_async_copy(
                    w_ref.at[which], held.at[pl.ds(place * width, width)], sems.at[1, place]
                )
            )
    for fetch in (*fetches, *row_fetches):
        fetch.start()
    total = None
    for i in range(groups):
        for fetch in fetches[4 * i : 4 * (i + 1)]:
            fetch.wait()
        both = jnp.concatenate([left[2 * i], left[2 * i + 1]], axis=1)
        term = jnp.dot(
            both, held[2 * i * width : 2 * (i + 1) * width], preferred_element_type=f32
        )
        total = term if total is None else total + term
    for fetch in row_fetches:
        fetch.wait()
    query = total[:tokens] + bias_ref[...]
    out_ref[...] = query
    scale_w = total[tokens : tokens + 1] + total[tokens + 1 : tokens + 2]
    shift_w = total[tokens + 2 : tokens + 3] + total[tokens + 3 : tokens + 4] + bias_ref[...]
    upstream = cot_ref[...].astype(f32) * gain_ref[...]
    terms = (
        query * query,
        upstream * query,
        query * scale_w,
        upstream * scale_w,
        query * shift_w,
        upstream * shift_w,
    )
    rows = []
    for term in terms:
        lanes = sum(term[:, k : k + 128] for k in range(0, cols, 128))
        rows.append(jnp.sum(jnp.transpose(lanes), axis=0, keepdims=True))
    rows.append(jnp.zeros((8 - len(rows), tokens), f32))
    sums_ref[...] = jnp.broadcast_to(jnp.concatenate(rows, axis=0)[None], sums_ref.shape)


def query_matmul(own, other, bias, gain, cotangent, weights):
    tokens, cols = cotangent.shape
    return pl.pallas_call(
        query_kernel,
        name="query",
        out_shape=(
            jax.ShapeDtypeStruct((tokens, cols), f32),
            jax.ShapeDtypeStruct((N_TP, 8, tokens), f32),
        ),
        in_specs=in_vmem(1) + [pl.BlockSpec(memory_space=pl.ANY)] * 5,
        out_specs=tuple(in_vmem(2)),
        scratch_shapes=[
            pltpu.VMEM((1, cols), f32),
            pltpu.VMEM((1, cols), f32),
            pltpu.VMEM((2 * own.shape[0],) + own.shape[1:], bf16),
            pltpu.VMEM((weights.shape[0] * weights.shape[1], cols), bf16),
            pltpu.SemaphoreType.DMA((2,)),
            pltpu.SemaphoreType.DMA((2, weights.shape[0])),
        ],
        compiler_params=pltpu.CompilerParams(vmem_limit_bytes=VMEM_LIMIT),
    )(cotangent, *in_hbm(bias[None], gain[None], own, other, weights))


def token_scales(sums_ref, query_width, width):
    sums = jnp.sum(sums_ref[...], axis=0)
    rinv = lax.rsqrt(sums[0:1] / query_width + epsilon)
    pull = sums[1:2] / query_width * rinv * rinv * rinv
    return across(rinv, width), across(pull, width)


def theirs_kernel(sums_ref, query_ref, gain_ref, cot_ref, w_ref, out_ref, grad_ref):
    core = 1 - lax.axis_index("c")
    cols = query_ref.shape[1]
    rinv, pull = token_scales(sums_ref, N_TP * cols, cols)
    upstream = cot_ref[...].astype(f32) * gain_ref[...]
    grad_ref[...] = (upstream * rinv - query_ref[...] * pull).astype(bf16)
    for i in range(out_ref.shape[0]):
        out_ref[i] = dot(grad_ref[...], w_ref[2 * i + core], ((1,), (1,))).astype(bf16)


def mine_kernel(sums_ref, query_ref, gain_ref, grad_ref, w_ref, out_ref, normed_ref):
    core = lax.axis_index("c")
    cols = query_ref.shape[1]
    for i in range(out_ref.shape[0]):
        out_ref[i] = dot(grad_ref[...], w_ref[2 * i + core], ((1,), (1,))).astype(bf16)
    rinv, _ = token_scales(sums_ref, N_TP * cols, cols)
    normed_ref[...] = (query_ref[...] * rinv * gain_ref[...]).astype(bf16)


def partial_matmul(kernel, name, sums, query, gain, last, weights):
    tokens, cols = query.shape
    groups, width = weights.shape[0] // 2, weights.shape[1]
    return pl.pallas_call(
        kernel,
        name=name,
        out_shape=(
            jax.ShapeDtypeStruct((groups, tokens, width), bf16),
            jax.ShapeDtypeStruct((tokens, cols), bf16),
        ),
        in_specs=in_vmem(5),
        out_specs=tuple(in_vmem(2)),
        compiler_params=pltpu.CompilerParams(vmem_limit_bytes=VMEM_LIMIT),
        cost_estimate=pl.CostEstimate(
            flops=2 * groups * tokens * cols * width,
            bytes_accessed=2 * groups * width * cols,
            transcendentals=0,
        ),
    )(sums, query, gain[None], last, weights)


def split(x):
    high = x.astype(bf16)
    return high, (x - high.astype(f32)).astype(bf16)


def back_kernel(
    sums_ref,
    inverse_ref,
    scale_ref,
    w_two_t_ref,
    pair_ref,
    normed_ref,
    select_ref,
    one_t_ref,
    pose_t_ref,
    w_three_hbm,
    slope_two_hbm,
    slope_one_hbm,
    slot_hbm,
    small_ref,
    w_three_ref,
    slope_two_ref,
    slope_one_ref,
    slot_ref,
    sems,
):
    far = (w_three_hbm, slope_two_hbm, slope_one_hbm)
    near = (w_three_ref, slope_two_ref, slope_one_ref)
    fetches = [
        pltpu.make_async_copy(source, target, sems.at[k])
        for k, (source, target) in enumerate(zip(far, near, strict=True))
    ]
    for fetch in fetches:
        fetch.start()
    width = normed_ref.shape[1]
    full = N_TP * width
    sums = jnp.sum(sums_ref[...], axis=0)
    sums = [sums[k : k + 1] for k in range(6)]
    rinv = lax.rsqrt(sums[0] / full + epsilon)
    pull = sums[1] / full * rinv * rinv * rinv
    grad_mean = (sums[3] * rinv - sums[2] * pull) / full
    grad_cross = ((sums[1] - sums[5]) * rinv - (sums[0] - sums[4]) * pull) / full
    total = sum(pair_ref[k].astype(f32) for k in range(pair_ref.shape[0]))
    normed_grad = total * (1.0 + scale_ref[...])
    latent_grad = across(inverse_ref[...], width) * (
        normed_grad - across(grad_mean, width) - normed_ref[...] * across(grad_cross, width)
    )
    slot_grad = dot(select_ref[...], latent_grad.astype(bf16), ((1,), (0,))).astype(bf16)
    slot_ref[...] = slot_grad
    store = pltpu.make_async_copy(slot_ref, slot_hbm, sems.at[len(fetches)])
    store.start()
    fetches[0].wait()
    two_grad = dot(slot_grad, w_three_ref[...], ((1,), (1,)))
    fetches[1].wait()
    two_grad = two_grad * slope_two_ref[...]
    fetches[2].wait()
    part = w_two_t_ref.shape[0]
    grad_two = jnp.zeros((part, part), f32)
    one_grad = []
    for k in range(two_grad.shape[1] // part):
        here = slice(k * part, (k + 1) * part)
        back_one = 0.0
        for piece in split(two_grad[:, here]):
            grad_two += jnp.dot(one_t_ref[here, :], piece, preferred_element_type=f32)
            back_one += jnp.dot(piece, w_two_t_ref[...], preferred_element_type=f32)
        one_grad.append(back_one * slope_one_ref[:, here])
    one_grad = jnp.concatenate(one_grad, axis=1)
    cross = sum(
        jnp.dot(pose_t_ref[...], piece, preferred_element_type=f32) for piece in split(one_grad)
    )
    cell = lax.broadcasted_iota(jnp.int32, cross.shape, 0) >> 4
    block = lax.broadcasted_iota(jnp.int32, cross.shape, 1) >> 5
    holds = (block & 8) + ((block & 2) << 1) + ((block & 4) >> 1) + (block & 1)
    cross = jnp.where(cell == holds, cross, 0.0)
    cross = sum(cross[16 * k : 16 * (k + 1)] for k in range(16))
    cross = sum(cross[:, 128 * k : 128 * (k + 1)] for k in range(4))
    cross = cross + pltpu.roll(cross, 64, 1)
    grad_one = cross + pltpu.roll(cross, 32, 1)
    rows_two, rows_one = part // N_TP, 16 // N_TP
    for k in range(N_TP):
        small_ref[k, :rows_two] = grad_two[k * rows_two : (k + 1) * rows_two]
        small_ref[k, rows_two:] = jnp.concatenate(
            [grad_one[k * rows_one : (k + 1) * rows_one], jnp.zeros((8 - rows_one, part), f32)]
        )
    store.wait()


def back(near, far):
    normed, select = near[5:7]
    part = near[3].shape[0]
    return pl.pallas_call(
        back_kernel,
        name="back",
        out_shape=(
            pltpu.HBM((select.shape[0], normed.shape[1]), bf16),
            jax.ShapeDtypeStruct((N_TP, part // N_TP + 8, part), f32),
        ),
        in_specs=in_vmem(len(near)) + [pl.BlockSpec(memory_space=pl.ANY)] * len(far),
        out_specs=(pl.BlockSpec(memory_space=pltpu.HBM), *in_vmem(1)),
        scratch_shapes=[pltpu.VMEM(x.shape, x.dtype) for x in far]
        + [
            pltpu.VMEM((select.shape[0], normed.shape[1]), bf16),
            pltpu.SemaphoreType.DMA((len(far) + 1,)),
        ],
        compiler_params=pltpu.CompilerParams(vmem_limit_bytes=VMEM_LIMIT),
    )(*near, *in_hbm(*far))


def three_kernel(slot_hbm, two_t_hbm, out_ref, slot_ref, two_t_ref, sems):
    fetches = (
        pltpu.make_async_copy(slot_hbm, slot_ref, sems.at[0]),
        pltpu.make_async_copy(two_t_hbm, two_t_ref, sems.at[1]),
    )
    for fetch in fetches:
        fetch.start()
    for fetch in fetches:
        fetch.wait()
    out_ref[...] = jnp.dot(
        two_t_ref[...], slot_ref[...], preferred_element_type=f32
    ).astype(out_ref.dtype)


def three(slot_grad, two_t):
    rows, slots = two_t.shape
    width = slot_grad.shape[1]
    return pl.pallas_call(
        three_kernel,
        name="three",
        out_shape=jax.ShapeDtypeStruct((rows, width), bf16),
        in_specs=[pl.BlockSpec(memory_space=pl.ANY)] * 2,
        out_specs=pl.BlockSpec(memory_space=pltpu.VMEM),
        scratch_shapes=[
            pltpu.VMEM(slot_grad.shape, bf16),
            pltpu.VMEM(two_t.shape, bf16),
            pltpu.SemaphoreType.DMA((2,)),
        ],
        compiler_params=pltpu.CompilerParams(vmem_limit_bytes=VMEM_LIMIT),
        cost_estimate=pl.CostEstimate(
            flops=2 * rows * slots * width, bytes_accessed=2 * rows * slots, transcendentals=0
        ),
    )(*in_hbm(slot_grad, two_t))


def unpack_kernel(small_ref, two_ref, one_ref):
    rows_two, rows_one = two_ref.shape[0] // N_TP, one_ref.shape[0] // N_TP
    for k in range(N_TP):
        two_ref[k * rows_two : (k + 1) * rows_two] = small_ref[k, :rows_two]
        one_ref[k * rows_one : (k + 1) * rows_one] = small_ref[
            k, rows_two : rows_two + rows_one, : one_ref.shape[1]
        ]


def unpack(small, cell_in, c_one, c_two):
    return pl.pallas_call(
        unpack_kernel,
        name="unpack",
        out_shape=(
            jax.ShapeDtypeStruct((c_two, c_two), f32),
            jax.ShapeDtypeStruct((cell_in, c_one), f32),
        ),
        in_specs=in_vmem(1),
        out_specs=tuple(in_vmem(2)),
        compiler_params=pltpu.CompilerParams(vmem_limit_bytes=VMEM_LIMIT),
    )(small)


def halves(x):
    high = lax.reduce_precision(x, 8, 7)
    return jnp.stack([high, x - high]).astype(bf16)


def swap_cores(x):
    return lax.ppermute(x, "c", [(0, 1), (1, 0)])


def body(
    latent,
    pose_rows,
    dest_device,
    dest_slot,
    w_section1,
    w_section2,
    w_section3,
    shift_mod,
    scale_mod,
    w_query,
    bias_query,
    gain_query,
    cotangent,
):
    tokens, width = latent.shape
    rows = pose_rows.shape[0]
    cols = w_query.shape[1]
    full_width = width * N_TP
    query_width = cols * N_TP
    slots = N_SEQ * CAP

    w_rows = copies(w_query, "x", N_X).reshape(N_X * w_query.shape[0], cols)
    w_rows, pose_rows, dest_device, dest_slot = lax.optimization_barrier(
        (w_rows, pose_rows, dest_device, dest_slot)
    )
    weights = lax.all_gather(w_rows, "z", axis=0, tiled=True).reshape(N_TP, width, cols)

    owner = dest_device[:, 0]
    marks = owner[:, None] == jnp.arange(N_SEQ, dtype=jnp.int32)[None, :]
    earlier = jnp.arange(rows)[:, None] > jnp.arange(rows)[None, :]
    before = dot(earlier.astype(bf16), marks.astype(bf16), ((1,), (0,)))
    rank = jnp.sum(jnp.where(marks, before, 0.0), axis=1).astype(jnp.int32)
    share = pose_rows.shape[1] // N_TP
    lane = jnp.arange(4 * share, dtype=jnp.int32)
    side, column = lane // (2 * share), lane % (2 * share)
    mine = lax.axis_index("y") * N_C + lax.axis_index("c")
    pick = (jnp.arange(pose_rows.shape[1])[:, None] == mine * share + column) & (column < share)
    line_data = dot(pose_rows, pick.astype(bf16), ((1,), (0,)))
    line_data = jnp.where(column == share, (dest_slot + 1).astype(f32)[:, None], line_data)
    line_data = jnp.where(side == rank[:, None] // (CAP // 2), line_data, 0.0).astype(bf16)
    line = owner * (CAP // 2) + rank % (CAP // 2)
    lines = slots // 2
    place = (jnp.arange(lines, dtype=jnp.int32)[:, None] == line[None, :]).astype(bf16)
    outgoing = dot(place, line_data, ((1,), (0,))).astype(bf16)
    incoming = exchange(outgoing.reshape(N_SEQ, CAP // 2, 4 * share), SEQ)
    incoming = incoming.reshape(lines, 4 * share)
    pieces = copies(incoming, TP, N_TP).transpose(1, 0, 2).reshape(lines, N_TP * 4 * share)
    source = jnp.arange(N_TP * 4 * share, dtype=jnp.int32)
    origin, source = source // (4 * share), source % (4 * share)
    to = jnp.where(
        source % (2 * share) < share,
        source // (2 * share) * N_TP * share + origin * share + source % (2 * share),
        -1,
    )
    order = (to[:, None] == jnp.arange(2 * N_TP * share, dtype=jnp.int32)[None, :]).astype(bf16)
    pose = dot(pieces, order, ((1,), (0,))).astype(bf16)
    pose = jnp.concatenate([pose[:, : N_TP * share], pose[:, N_TP * share :]])
    slot = jnp.concatenate(
        [incoming[:, share : share + 1], incoming[:, 3 * share : 3 * share + 1]]
    ).astype(jnp.int32) - 1
    select = (slot == jnp.arange(tokens, dtype=jnp.int32)[None, :]).astype(bf16)

    cell_in, c_one = w_section1.shape
    c_two = w_section2.shape[1]
    in_cell = jnp.arange(16 * cell_in) // cell_in
    out_cell = jnp.arange(16 * c_one) // c_one
    big_i, big_j, a, b = out_cell // 8, (out_cell // 4) % 2, (out_cell // 2) % 2, out_cell % 2
    from_cell = 4 * (2 * big_i + a) + 2 * big_j + b
    cell_mask = in_cell[:, None] == from_cell[None, :]
    w_one = jnp.where(cell_mask, jnp.tile(w_section1, (16, 16)), jnp.zeros((), bf16))
    quad = jnp.arange(4 * c_two) // c_two
    w_two = jnp.where(
        quad[:, None] == quad[None, :], jnp.tile(w_section2, (4, 4)), jnp.zeros((), bf16)
    )
    z_one = dot(pose, w_one, ((1,), (0,)))
    stacked_one = jax.nn.silu(z_one).astype(bf16)
    z_two = dot(stacked_one, w_two, ((1,), (0,)))
    stacked_two = jax.nn.silu(z_two).astype(bf16)
    pose_tokens = dot(stacked_two, w_section3, ((1,), (0,))).astype(bf16)
    guidance = dot(select, pose_tokens, ((0,), (0,)))
    summed = latent.astype(f32) + guidance

    local_mean = jnp.mean(summed, axis=1)
    local_square = jnp.sum((summed - local_mean[:, None]) ** 2, axis=1)
    stats = copies(jnp.stack([local_mean, local_square]), TP, N_TP)
    center = jnp.mean(stats[:, 0], axis=0)
    spread = (
        jnp.sum(stats[:, 1], axis=0) + width * jnp.sum((stats[:, 0] - center) ** 2, axis=0)
    ) / full_width
    inverse = lax.rsqrt(spread + epsilon)[:, None]
    normed = (summed - center[:, None]) * inverse
    modulated = (normed * (1.0 + scale_mod) + shift_mod).astype(bf16)
    extra = jnp.concatenate([halves(1.0 + scale_mod), halves(shift_mod)])
    extra = jnp.pad(extra, ((0, 12), (0, 0)))
    own = copies(jnp.concatenate([modulated, extra]), "y", N_Y)
    per = stacked_two.shape[1] // N_SEQ
    row = jnp.arange(stacked_two.shape[1], dtype=jnp.int32)
    leaves = row // per % N_X * (N_Z * per) + row // (per * N_X) * per + row % per
    order = (leaves[:, None] == row[None, :]).astype(bf16)
    ready = (
        normed,
        inverse.reshape(1, tokens),
        select,
        dot(order, stacked_two, ((0,), (1,))).astype(bf16),
        silu_slope(z_two),
        stacked_one.T,
        silu_slope(z_one),
        pose.T,
        w_section2.T,
    )
    ready, own = lax.optimization_barrier((ready, own))
    normed, inverse, select, leaving_two, slope_two, one_t, slope_one, pose_t, w_two_t = ready
    other = swap_cores(own)

    query, sums = query_matmul(own, other, bias_query, gain_query, cotangent, weights)
    sums = exchange(sums, TP)
    theirs, query_grad = partial_matmul(
        theirs_kernel, "theirs", sums, query, gain_query, cotangent, weights
    )
    theirs = swap_cores(theirs)
    mine, normed_query = partial_matmul(
        mine_kernel, "mine", sums, query, gain_query, query_grad, weights
    )
    pair = (mine.astype(f32) + theirs.astype(f32)).astype(bf16)
    pair = exchange(pair, "y")
    slot_grad, small = back(
        (sums, inverse, scale_mod[None], w_two_t, pair, normed, select, one_t, pose_t),
        (w_section3, slope_two, slope_one),
    )
    grad_three = three(slot_grad, leaving_two)

    small = jnp.sum(exchange(small, TP), axis=0).astype(bf16)
    wide = small.shape[0] // per * c_two
    small = jnp.concatenate([small[k : k + per] for k in range(0, small.shape[0], per)], axis=1)
    small = jnp.pad(small, ((0, 0), (0, width - wide)))
    shares = jnp.concatenate(
        [
            grad_three.reshape(N_X, N_Z * per, width),
            jnp.broadcast_to(small[None], (N_X, per, width)),
        ],
        axis=1,
    )
    shares = jnp.sum(exchange(shares, "x").astype(f32), axis=0).astype(bf16)
    shares = jnp.concatenate(
        [
            shares[: N_Z * per].reshape(N_Z, per, width),
            jnp.broadcast_to(shares[None, N_Z * per :, :wide], (N_Z, per, wide)),
        ],
        axis=2,
    )
    total = jnp.sum(exchange(shares, "z").astype(f32), axis=0)
    section_three_grad = total[:, :width]
    small = [total[:, k : k + c_two] for k in range(width, width + wide, c_two)]
    small = copies(jnp.concatenate(small), TP, N_TP)
    section_two_grad, section_one_grad = unpack(small, cell_in, c_one, c_two)
    return (normed_query, section_three_grad, section_two_grad, section_one_grad)


def solution(mesh):
    fine = Mesh(mesh.devices.reshape(N_Z, N_X, N_Y, N_C), ("z", "x", "y", "c"))
    return jax.shard_map(
        body,
        mesh=fine,
        in_specs=(
            P(SEQ, TP),
            P(SEQ, None),
            P(SEQ, None),
            P(SEQ),
            P(),
            P(),
            P(None, TP),
            P(TP),
            P(TP),
            P(SEQ, TP),
            P(TP),
            P(TP),
            P(SEQ, TP),
        ),
        out_specs=(P(SEQ, TP), P(SEQ, TP), P(), P()),
        check_vma=False,
    )
```

```python
import jax
import jax.numpy as jnp
from jax import lax
from jax.experimental import pallas as pl
from jax.experimental.pallas import tpu as pltpu
from jax.sharding import Mesh, PartitionSpec as P

epsilon = 1e-06
bf16 = jnp.bfloat16
f32 = jnp.float32
SEQ = ("z", "x")
TP = ("y", "c")
N_Z, N_X, N_Y, N_C = 16, 4, 4, 2
N_SEQ, N_TP = N_Z * N_X, N_Y * N_C
CAP = 8


def silu_slope(z):
    s = jax.nn.sigmoid(z)
    return s * (1.0 + z * (1.0 - s))


def dot(a, b, dims, precision=None):
    return lax.dot_general(a, b, (dims, ((), ())), precision=precision, preferred_element_type=f32)


def exchange(x, axis):
    return lax.all_to_all(x, axis, split_axis=0, concat_axis=0, tiled=True)


def copies(x, axis, count):
    return exchange(jnp.broadcast_to(x[None], (count,) + x.shape), axis)


VMEM_LIMIT = 24 * 1024 * 1024


def in_vmem(count):
    return [pl.BlockSpec(memory_space=pltpu.VMEM)] * count


def in_hbm(*arrays):
    return tuple(pltpu.with_memory_space_constraint(x, pltpu.HBM) for x in arrays)


def across(column, width):
    block = jnp.transpose(jnp.broadcast_to(column, (128, column.shape[1])))
    return jnp.concatenate([block] * (width // 128), axis=1)


def query_kernel(
    cot_ref,
    bias_hbm,
    gain_hbm,
    own_ref,
    other_ref,
    w_ref,
    out_ref,
    sums_ref,
    held,
    bias_ref,
    gain_ref,
    left,
    row_sems,
    sems,
):
    core = lax.axis_index("c")
    row_fetches = (
        pltpu.make_async_copy(bias_hbm, bias_ref, row_sems.at[0]),
        pltpu.make_async_copy(gain_hbm, gain_ref, row_sems.at[1]),
    )
    groups, _, width = own_ref.shape
    tokens, cols = out_ref.shape
    fetches = []
    for i in range(groups):
        for k, (source, which) in enumerate(
            ((own_ref, 2 * i + core), (other_ref, 2 * i + 1 - core))
        ):
            place = 2 * i + k
            fetches.append(pltpu.make_async_copy(source.at[i], left.at[place], sems.at[0, place]))
            fetches.append(
                pltpu.make_async_copy(
                    w_ref.at[which], held.at[pl.ds(place * width, width)], sems.at[1, place]
                )
            )
    for fetch in (*fetches, *row_fetches):
        fetch.start()
    total = None
    for i in range(groups):
        for fetch in fetches[4 * i : 4 * (i + 1)]:
            fetch.wait()
        both = jnp.concatenate([left[2 * i], left[2 * i + 1]], axis=1)
        term = jnp.dot(
            both, held[2 * i * width : 2 * (i + 1) * width], preferred_element_type=f32
        )
        total = term if total is None else total + term
    for fetch in row_fetches:
        fetch.wait()
    query = total[:tokens] + bias_ref[...]
    out_ref[...] = query
    scale_w = total[tokens : tokens + 1] + total[tokens + 1 : tokens + 2]
    shift_w = total[tokens + 2 : tokens + 3] + total[tokens + 3 : tokens + 4] + bias_ref[...]
    upstream = cot_ref[...].astype(f32) * gain_ref[...]
    terms = (
        query * query,
        upstream * query,
        query * scale_w,
        upstream * scale_w,
        query * shift_w,
        upstream * shift_w,
    )
    rows = []
    for term in terms:
        lanes = sum(term[:, k : k + 128] for k in range(0, cols, 128))
        rows.append(jnp.sum(jnp.transpose(lanes), axis=0, keepdims=True))
    rows.append(jnp.zeros((8 - len(rows), tokens), f32))
    sums_ref[...] = jnp.broadcast_to(jnp.concatenate(rows, axis=0)[None], sums_ref.shape)


def query_matmul(own, other, bias, gain, cotangent, weights):
    tokens, cols = cotangent.shape
    return pl.pallas_call(
        query_kernel,
        name="query",
        out_shape=(
            jax.ShapeDtypeStruct((tokens, cols), f32),
            jax.ShapeDtypeStruct((N_TP, 8, tokens), f32),
            pltpu.VMEM((weights.shape[0] * weights.shape[1], cols), bf16),
        ),
        in_specs=in_vmem(1) + [pl.BlockSpec(memory_space=pl.ANY)] * 5,
        out_specs=tuple(in_vmem(3)),
        scratch_shapes=[
            pltpu.VMEM((1, cols), f32),
            pltpu.VMEM((1, cols), f32),
            pltpu.VMEM((2 * own.shape[0],) + own.shape[1:], bf16),
            pltpu.SemaphoreType.DMA((2,)),
            pltpu.SemaphoreType.DMA((2, weights.shape[0])),
        ],
        compiler_params=pltpu.CompilerParams(vmem_limit_bytes=VMEM_LIMIT),
    )(cotangent, *in_hbm(bias[None], gain[None], own, other, weights))


def token_scales(sums_ref, query_width, width):
    sums = jnp.sum(sums_ref[...], axis=0)
    rinv = lax.rsqrt(sums[0:1] / query_width + epsilon)
    pull = sums[1:2] / query_width * rinv * rinv * rinv
    return across(rinv, width), across(pull, width)


def theirs_kernel(sums_ref, query_ref, gain_ref, cot_ref, w_ref, out_ref, grad_ref):
    cols = query_ref.shape[1]
    rinv, pull = token_scales(sums_ref, N_TP * cols, cols)
    upstream = cot_ref[...].astype(f32) * gain_ref[...]
    grad_ref[...] = (upstream * rinv - query_ref[...] * pull).astype(bf16)
    for i in range(out_ref.shape[0]):
        out_ref[i] = dot(grad_ref[...], w_ref[2 * i + 1], ((1,), (1,))).astype(bf16)


def mine_kernel(sums_ref, query_ref, gain_ref, grad_ref, w_ref, out_ref, normed_ref):
    cols = query_ref.shape[1]
    for i in range(out_ref.shape[0]):
        out_ref[i] = dot(grad_ref[...], w_ref[2 * i], ((1,), (1,))).astype(bf16)
    rinv, _ = token_scales(sums_ref, N_TP * cols, cols)
    normed_ref[...] = (query_ref[...] * rinv * gain_ref[...]).astype(bf16)


def partial_matmul(kernel, name, sums, query, gain, last, weights):
    tokens, cols = query.shape
    groups, width = weights.shape[0] // 2, weights.shape[1]
    return pl.pallas_call(
        kernel,
        name=name,
        out_shape=(
            jax.ShapeDtypeStruct((groups, tokens, width), bf16),
            jax.ShapeDtypeStruct((tokens, cols), bf16),
        ),
        in_specs=in_vmem(5),
        out_specs=tuple(in_vmem(2)),
        compiler_params=pltpu.CompilerParams(vmem_limit_bytes=VMEM_LIMIT),
        cost_estimate=pl.CostEstimate(
            flops=2 * groups * tokens * cols * width,
            bytes_accessed=2 * groups * width * cols,
            transcendentals=0,
        ),
    )(sums, query, gain[None], last, weights)


def split(x):
    high = x.astype(bf16)
    return high, (x - high.astype(f32)).astype(bf16)


def back_kernel(
    sums_ref,
    inverse_ref,
    scale_ref,
    w_two_t_ref,
    pair_ref,
    normed_ref,
    select_ref,
    one_t_ref,
    pose_t_ref,
    w_three_hbm,
    slope_two_hbm,
    slope_one_hbm,
    slot_hbm,
    small_ref,
    w_three_ref,
    slope_two_ref,
    slope_one_ref,
    slot_ref,
    sems,
):
    far = (w_three_hbm, slope_two_hbm, slope_one_hbm)
    near = (w_three_ref, slope_two_ref, slope_one_ref)
    fetches = [
        pltpu.make_async_copy(source, target, sems.at[k])
        for k, (source, target) in enumerate(zip(far, near, strict=True))
    ]
    for fetch in fetches:
        fetch.start()
    width = normed_ref.shape[1]
    full = N_TP * width
    sums = jnp.sum(sums_ref[...], axis=0)
    sums = [sums[k : k + 1] for k in range(6)]
    rinv = lax.rsqrt(sums[0] / full + epsilon)
    pull = sums[1] / full * rinv * rinv * rinv
    grad_mean = (sums[3] * rinv - sums[2] * pull) / full
    grad_cross = ((sums[1] - sums[5]) * rinv - (sums[0] - sums[4]) * pull) / full
    total = sum(pair_ref[k].astype(f32) for k in range(pair_ref.shape[0]))
    normed_grad = total * (1.0 + scale_ref[...])
    latent_grad = across(inverse_ref[...], width) * (
        normed_grad - across(grad_mean, width) - normed_ref[...] * across(grad_cross, width)
    )
    slot_grad = dot(select_ref[...], latent_grad.astype(bf16), ((1,), (0,))).astype(bf16)
    slot_ref[...] = slot_grad
    store = pltpu.make_async_copy(slot_ref, slot_hbm, sems.at[len(fetches)])
    store.start()
    fetches[0].wait()
    two_grad = dot(slot_grad, w_three_ref[...], ((1,), (1,)))
    fetches[1].wait()
    two_grad = two_grad * slope_two_ref[...]
    fetches[2].wait()
    part = w_two_t_ref.shape[0]
    grad_two = jnp.zeros((part, part), f32)
    one_grad = []
    for k in range(two_grad.shape[1] // part):
        here = slice(k * part, (k + 1) * part)
        back_one = 0.0
        for piece in split(two_grad[:, here]):
            grad_two += jnp.dot(one_t_ref[here, :], piece, preferred_element_type=f32)
            back_one += jnp.dot(piece, w_two_t_ref[...], preferred_element_type=f32)
        one_grad.append(back_one * slope_one_ref[:, here])
    one_grad = jnp.concatenate(one_grad, axis=1)
    cross = sum(
        jnp.dot(pose_t_ref[...], piece, preferred_element_type=f32) for piece in split(one_grad)
    )
    cell = lax.broadcasted_iota(jnp.int32, cross.shape, 0) >> 4
    block = lax.broadcasted_iota(jnp.int32, cross.shape, 1) >> 5
    holds = (block & 8) + ((block & 2) << 1) + ((block & 4) >> 1) + (block & 1)
    cross = jnp.where(cell == holds, cross, 0.0)
    cross = sum(cross[16 * k : 16 * (k + 1)] for k in range(16))
    cross = sum(cross[:, 128 * k : 128 * (k + 1)] for k in range(4))
    cross = cross + pltpu.roll(cross, 64, 1)
    grad_one = cross + pltpu.roll(cross, 32, 1)
    rows_two, rows_one = part // N_TP, 16 // N_TP
    for k in range(N_TP):
        small_ref[k, :rows_two] = grad_two[k * rows_two : (k + 1) * rows_two]
        small_ref[k, rows_two:] = jnp.concatenate(
            [grad_one[k * rows_one : (k + 1) * rows_one], jnp.zeros((8 - rows_one, part), f32)]
        )
    store.wait()


def back(near, far):
    normed, select = near[5:7]
    part = near[3].shape[0]
    return pl.pallas_call(
        back_kernel,
        name="back",
        out_shape=(
            pltpu.HBM((select.shape[0], normed.shape[1]), bf16),
            jax.ShapeDtypeStruct((N_TP, part // N_TP + 8, part), f32),
        ),
        in_specs=in_vmem(len(near)) + [pl.BlockSpec(memory_space=pl.ANY)] * len(far),
        out_specs=(pl.BlockSpec(memory_space=pltpu.HBM), *in_vmem(1)),
        scratch_shapes=[pltpu.VMEM(x.shape, x.dtype) for x in far]
        + [
            pltpu.VMEM((select.shape[0], normed.shape[1]), bf16),
            pltpu.SemaphoreType.DMA((len(far) + 1,)),
        ],
        compiler_params=pltpu.CompilerParams(vmem_limit_bytes=VMEM_LIMIT),
    )(*near, *in_hbm(*far))


def three_kernel(slot_hbm, two_t_hbm, out_ref, slot_ref, two_t_ref, sems):
    fetches = (
        pltpu.make_async_copy(slot_hbm, slot_ref, sems.at[0]),
        pltpu.make_async_copy(two_t_hbm, two_t_ref, sems.at[1]),
    )
    for fetch in fetches:
        fetch.start()
    for fetch in fetches:
        fetch.wait()
    out_ref[...] = jnp.dot(
        two_t_ref[...], slot_ref[...], preferred_element_type=f32
    ).astype(out_ref.dtype)


def three(slot_grad, two_t):
    rows, slots = two_t.shape
    width = slot_grad.shape[1]
    return pl.pallas_call(
        three_kernel,
        name="three",
        out_shape=jax.ShapeDtypeStruct((rows, width), bf16),
        in_specs=[pl.BlockSpec(memory_space=pl.ANY)] * 2,
        out_specs=pl.BlockSpec(memory_space=pltpu.VMEM),
        scratch_shapes=[
            pltpu.VMEM(slot_grad.shape, bf16),
            pltpu.VMEM(two_t.shape, bf16),
            pltpu.SemaphoreType.DMA((2,)),
        ],
        compiler_params=pltpu.CompilerParams(vmem_limit_bytes=VMEM_LIMIT),
        cost_estimate=pl.CostEstimate(
            flops=2 * rows * slots * width, bytes_accessed=2 * rows * slots, transcendentals=0
        ),
    )(*in_hbm(slot_grad, two_t))


def unpack_kernel(small_ref, two_ref, one_ref):
    rows_two, rows_one = two_ref.shape[0] // N_TP, one_ref.shape[0] // N_TP
    for k in range(N_TP):
        two_ref[k * rows_two : (k + 1) * rows_two] = small_ref[k, :rows_two]
        one_ref[k * rows_one : (k + 1) * rows_one] = small_ref[
            k, rows_two : rows_two + rows_one, : one_ref.shape[1]
        ]


def unpack(small, cell_in, c_one, c_two):
    return pl.pallas_call(
        unpack_kernel,
        name="unpack",
        out_shape=(
            jax.ShapeDtypeStruct((c_two, c_two), f32),
            jax.ShapeDtypeStruct((cell_in, c_one), f32),
        ),
        in_specs=in_vmem(1),
        out_specs=tuple(in_vmem(2)),
        compiler_params=pltpu.CompilerParams(vmem_limit_bytes=VMEM_LIMIT),
    )(small)


def halves(x):
    high = lax.reduce_precision(x, 8, 7)
    return jnp.stack([high, x - high]).astype(bf16)


def swap_cores(x):
    return lax.ppermute(x, "c", [(0, 1), (1, 0)])


def body(
    latent,
    pose_rows,
    dest_device,
    dest_slot,
    w_section1,
    w_section2,
    w_section3,
    shift_mod,
    scale_mod,
    w_query,
    bias_query,
    gain_query,
    cotangent,
):
    tokens, width = latent.shape
    rows = pose_rows.shape[0]
    cols = w_query.shape[1]
    full_width = width * N_TP
    query_width = cols * N_TP
    slots = N_SEQ * CAP

    w_rows = copies(w_query, "x", N_X).reshape(N_X * w_query.shape[0], cols)
    w_rows, pose_rows, dest_device, dest_slot = lax.optimization_barrier(
        (w_rows, pose_rows, dest_device, dest_slot)
    )
    weights = lax.all_gather(w_rows, "z", axis=0, tiled=True).reshape(N_TP, width, cols)

    owner = dest_device[:, 0]
    marks = owner[:, None] == jnp.arange(N_SEQ, dtype=jnp.int32)[None, :]
    earlier = jnp.arange(rows)[:, None] > jnp.arange(rows)[None, :]
    before = dot(earlier.astype(bf16), marks.astype(bf16), ((1,), (0,)))
    rank = jnp.sum(jnp.where(marks, before, 0.0), axis=1).astype(jnp.int32)
    share = pose_rows.shape[1] // N_TP
    lane = jnp.arange(4 * share, dtype=jnp.int32)
    side, column = lane // (2 * share), lane % (2 * share)
    mine = lax.axis_index("y") * N_C + lax.axis_index("c")
    pick = (jnp.arange(pose_rows.shape[1])[:, None] == mine * share + column) & (column < share)
    line_data = dot(pose_rows, pick.astype(bf16), ((1,), (0,)))
    line_data = jnp.where(column == share, (dest_slot + 1).astype(f32)[:, None], line_data)
    line_data = jnp.where(side == rank[:, None] // (CAP // 2), line_data, 0.0).astype(bf16)
    line = owner * (CAP // 2) + rank % (CAP // 2)
    lines = slots // 2
    place = (jnp.arange(lines, dtype=jnp.int32)[:, None] == line[None, :]).astype(bf16)
    outgoing = dot(place, line_data, ((1,), (0,))).astype(bf16)
    incoming = exchange(outgoing.reshape(N_SEQ, CAP // 2, 4 * share), SEQ)
    incoming = incoming.reshape(lines, 4 * share)
    pieces = copies(incoming, TP, N_TP).transpose(1, 0, 2).reshape(lines, N_TP * 4 * share)
    source = jnp.arange(N_TP * 4 * share, dtype=jnp.int32)
    origin, source = source // (4 * share), source % (4 * share)
    to = jnp.where(
        source % (2 * share) < share,
        source // (2 * share) * N_TP * share + origin * share + source % (2 * share),
        -1,
    )
    order = (to[:, None] == jnp.arange(2 * N_TP * share, dtype=jnp.int32)[None, :]).astype(bf16)
    pose = dot(pieces, order, ((1,), (0,))).astype(bf16)
    pose = jnp.concatenate([pose[:, : N_TP * share], pose[:, N_TP * share :]])
    slot = jnp.concatenate(
        [incoming[:, share : share + 1], incoming[:, 3 * share : 3 * share + 1]]
    ).astype(jnp.int32) - 1
    select = (slot == jnp.arange(tokens, dtype=jnp.int32)[None, :]).astype(bf16)

    cell_in, c_one = w_section1.shape
    c_two = w_section2.shape[1]
    in_cell = jnp.arange(16 * cell_in) // cell_in
    out_cell = jnp.arange(16 * c_one) // c_one
    big_i, big_j, a, b = out_cell // 8, (out_cell // 4) % 2, (out_cell // 2) % 2, out_cell % 2
    from_cell = 4 * (2 * big_i + a) + 2 * big_j + b
    cell_mask = in_cell[:, None] == from_cell[None, :]
    w_one = jnp.where(cell_mask, jnp.tile(w_section1, (16, 16)), jnp.zeros((), bf16))
    quad = jnp.arange(4 * c_two) // c_two
    w_two = jnp.where(
        quad[:, None] == quad[None, :], jnp.tile(w_section2, (4, 4)), jnp.zeros((), bf16)
    )
    z_one = dot(pose, w_one, ((1,), (0,)))
    stacked_one = jax.nn.silu(z_one).astype(bf16)
    z_two = dot(stacked_one, w_two, ((1,), (0,)))
    stacked_two = jax.nn.silu(z_two).astype(bf16)
    pose_tokens = dot(stacked_two, w_section3, ((1,), (0,))).astype(bf16)
    guidance = dot(select, pose_tokens, ((0,), (0,)))
    summed = latent.astype(f32) + guidance

    local_mean = jnp.mean(summed, axis=1)
    local_square = jnp.sum((summed - local_mean[:, None]) ** 2, axis=1)
    stats = copies(jnp.stack([local_mean, local_square]), TP, N_TP)
    center = jnp.mean(stats[:, 0], axis=0)
    spread = (
        jnp.sum(stats[:, 1], axis=0) + width * jnp.sum((stats[:, 0] - center) ** 2, axis=0)
    ) / full_width
    inverse = lax.rsqrt(spread + epsilon)[:, None]
    normed = (summed - center[:, None]) * inverse
    modulated = (normed * (1.0 + scale_mod) + shift_mod).astype(bf16)
    extra = jnp.concatenate([halves(1.0 + scale_mod), halves(shift_mod)])
    extra = jnp.pad(extra, ((0, 12), (0, 0)))
    own = copies(jnp.concatenate([modulated, extra]), "y", N_Y)
    per = stacked_two.shape[1] // N_SEQ
    row = jnp.arange(stacked_two.shape[1], dtype=jnp.int32)
    leaves = row // per % N_X * (N_Z * per) + row // (per * N_X) * per + row % per
    order = (leaves[:, None] == row[None, :]).astype(bf16)
    ready = (
        normed,
        inverse.reshape(1, tokens),
        select,
        dot(order, stacked_two, ((0,), (1,))).astype(bf16),
        silu_slope(z_two),
        stacked_one.T,
        silu_slope(z_one),
        pose.T,
        w_section2.T,
    )
    ready, own = lax.optimization_barrier((ready, own))
    normed, inverse, select, leaving_two, slope_two, one_t, slope_one, pose_t, w_two_t = ready
    other = swap_cores(own)

    query, sums, held = query_matmul(own, other, bias_query, gain_query, cotangent, weights)
    weights = held.reshape(weights.shape)
    sums = exchange(sums, TP)
    theirs, query_grad = partial_matmul(
        theirs_kernel, "theirs", sums, query, gain_query, cotangent, weights
    )
    theirs = swap_cores(theirs)
    mine, normed_query = partial_matmul(
        mine_kernel, "mine", sums, query, gain_query, query_grad, weights
    )
    pair = (mine.astype(f32) + theirs.astype(f32)).astype(bf16)
    pair = exchange(pair, "y")
    slot_grad, small = back(
        (sums, inverse, scale_mod[None], w_two_t, pair, normed, select, one_t, pose_t),
        (w_section3, slope_two, slope_one),
    )
    grad_three = three(slot_grad, leaving_two)

    small = jnp.sum(exchange(small, TP), axis=0).astype(bf16)
    wide = small.shape[0] // per * c_two
    small = jnp.concatenate([small[k : k + per] for k in range(0, small.shape[0], per)], axis=1)
    small = jnp.pad(small, ((0, 0), (0, width - wide)))
    shares = jnp.concatenate(
        [
            grad_three.reshape(N_X, N_Z * per, width),
            jnp.broadcast_to(small[None], (N_X, per, width)),
        ],
        axis=1,
    )
    shares = jnp.sum(exchange(shares, "x").astype(f32), axis=0).astype(bf16)
    shares = jnp.concatenate(
        [
            shares[: N_Z * per].reshape(N_Z, per, width),
            jnp.broadcast_to(shares[None, N_Z * per :, :wide], (N_Z, per, wide)),
        ],
        axis=2,
    )
    total = jnp.sum(exchange(shares, "z").astype(f32), axis=0)
    section_three_grad = total[:, :width]
    small = [total[:, k : k + c_two] for k in range(width, width + wide, c_two)]
    small = copies(jnp.concatenate(small), TP, N_TP)
    section_two_grad, section_one_grad = unpack(small, cell_in, c_one, c_two)
    return (normed_query, section_three_grad, section_two_grad, section_one_grad)


def solution(mesh):
    fine = Mesh(mesh.devices.reshape(N_Z, N_X, N_Y, N_C), ("z", "x", "y", "c"))
    return jax.shard_map(
        body,
        mesh=fine,
        in_specs=(
            P(SEQ, TP),
            P(SEQ, None),
            P(SEQ, None),
            P(SEQ),
            P(),
            P(),
            P(None, TP),
            P(TP),
            P(TP),
            P(SEQ, TP),
            P(TP),
            P(TP),
            P(SEQ, TP),
        ),
        out_specs=(P(SEQ, TP), P(SEQ, TP), P(), P()),
        check_vma=False,
    )
```
